32 devices in a mesh: group: 2 (over core), expert: 8 (over z, y), dp: 2 (over x).
Axes of the slice: x: 2, y: 2, z: 4, core: 2. Of those that a mesh axis runs over, the one named last changes fastest.
Arguments:
- tokens: bfloat16 [512, 5120], P(('group', 'expert'), 'dp'), may hold values from -6 to 6
- grad_out: bfloat16 [512, 5120], P(('group', 'expert'), 'dp'), may hold values from -6 to 6
- expert_ids: int32 [512, 8], replicated, may hold values from 0 to 15, as said below
- gate_score: float32 [512, 8], replicated, may hold values from -6 to 6
- w_gate_up: bfloat16 [16, 5120, 2, 1024], P(('group', 'expert'), 'dp'), may hold values from -0.078125 to 0.078125
- w_down: bfloat16 [16, 1024, 5120], P(('group', 'expert'), None, 'dp'), may hold values from -0.1875 to 0.1875
Outputs:
- layer_out: bfloat16 [512, 5120], P(('group', 'expert'), 'dp')
- grad_in: bfloat16 [512, 5120], P(('group', 'expert'), 'dp')
The draws below stay inside these ranges and needn't reach their ends.
Inputs may be any that keep to these rules, and one draw needn't show every extreme that they name: `expert_ids`: each row names 8 distinct experts, expert number = group * 8 + index, lying in exactly 1 group with 8 experts in each, listed by rising group. In every aligned block of 32 rows each group is named by exactly half of the rows. For a group g and an index e, among the rows of the blocks numbered j * 8 + e (j from 0 to 1) that name group g, no expert of g is named more than 32 times, and some expert of g exactly 32 times.
All inputs are finite; a program needn't handle non-finite values.
Results may differ from the reference program's by a relative error of at most 0.0057.
Values may be sent and summed in bfloat16 or wider, within the bound.
A program may use at most 64 MiB of HBM per device.

```python
import jax
import jax.numpy as jnp
from jax import lax

D = 5120
H = 1024
TOPK = 8
TOK_DEV = 32
EXPERTS = 16
TOKENS = 512
CAP = 32
N_GROUP = 2
N_EXPERT = 8


def block_loads(key):
    key_perm, key_steps = jax.random.split(key)
    labels = jax.random.permutation(key_perm, N_EXPERT)
    load_counts = jnp.zeros((N_EXPERT,), jnp.int32).at[labels[0]].set(CAP)
    pick_total = TOK_DEV * TOPK
    random_pairs = jax.random.randint(key_steps, (pick_total - CAP + 1, 2), 0, N_EXPERT)

    def add_one(position, counts_now):
        chosen = labels[jnp.minimum(random_pairs[position, 0], random_pairs[position, 1])]
        is_full = counts_now[chosen] >= CAP
        chosen = jnp.where(is_full, jnp.argmin(counts_now), chosen)
        return counts_now.at[chosen].add(1)
    return lax.fori_loop(0, pick_total - CAP, add_one, load_counts)


def block_experts(key):
    key_load, key_rows = jax.random.split(key)
    load_counts = block_loads(key_load)
    row_total = N_GROUP * (TOK_DEV // 2)
    per_group = TOPK * 2 // N_GROUP
    run_ends = jnp.cumsum(load_counts)
    positions = jnp.arange(row_total * per_group, dtype=jnp.int32)
    expert = jnp.sum((run_ends[None, :] <= positions[:, None]).astype(jnp.int32), axis=1)
    pick_table = expert.reshape(per_group, row_total)
    row_order = jax.random.permutation(key_rows, row_total)
    return jnp.zeros((row_total, per_group), jnp.int32).at[row_order].set(pick_table.T)


def column_visits(key):
    key_perm, key_side = jax.random.split(key)
    shuffle = jax.random.permutation(key_perm, N_GROUP)
    side_keys = jax.random.split(key_side, N_GROUP // 2)
    chosen_side = jax.vmap(jax.random.permutation, in_axes=(0, None))(side_keys, TOK_DEV) < TOK_DEV // 2
    chosen = jnp.where(chosen_side, shuffle[0::2][:, None], shuffle[1::2][:, None])
    group_range = jnp.arange(N_GROUP, dtype=jnp.int32)
    return jnp.sum((chosen[:, :, None] == group_range).astype(jnp.int32), axis=0)


def draw_expert_ids(key, part):
    key_vis, key_blocks = jax.random.split(jax.random.fold_in(key, 7))
    columns = N_GROUP * N_EXPERT
    visitors = TOK_DEV // 2
    row_total = N_GROUP * visitors
    per_group = TOPK * 2 // N_GROUP
    visits = jax.vmap(column_visits)(jax.random.split(key_vis, columns))
    experts = jax.vmap(block_experts)(jax.random.split(key_blocks, columns)).reshape(N_GROUP, N_EXPERT, row_total, per_group)
    slot_index = jnp.maximum(jnp.cumsum(visits, axis=1) - 1, 0)
    column_range = jnp.arange(columns, dtype=jnp.int32)
    source_group = column_range // N_EXPERT
    source_index = column_range % N_EXPERT
    row_index = source_group[:, None, None] * visitors + slot_index
    target_group = jnp.arange(N_GROUP, dtype=jnp.int32)[None, None, :]
    picked = experts[target_group, source_index[:, None, None], row_index]
    global_ids = target_group[..., None] * N_EXPERT + picked
    visit_order = jnp.argsort(1 - visits, axis=2, stable=True)[:, :, :N_GROUP // 2]
    visit_index = jnp.broadcast_to(visit_order[..., None], (columns, TOK_DEV, N_GROUP // 2, per_group))
    chosen = jnp.take_along_axis(global_ids, visit_index, axis=2)
    return chosen.reshape(columns * TOK_DEV, TOPK).astype(jnp.int32)


def levels(rng, shape, shards, low, largest):
    def one(axis_at, blocks):
        draws = jax.random.uniform(jax.random.fold_in(jax.random.fold_in(rng, 6), axis_at), (blocks,), jnp.float32, low / len(shards), largest / len(shards))
        return jnp.repeat(jnp.exp(draws), shape[axis_at] // blocks).reshape((-1,) + (1,) * (len(shape) - axis_at - 1))

    factor_of = one(*shards[0])
    for cut in shards[1:]:
        factor_of = factor_of * one(*cut)
    return factor_of


def noise(rng, dims, deviation, bound, shards=(), kind=jnp.bfloat16):
    gain = levels(rng, dims, shards, -0.22, 0.18) if shards else 1.0
    values = jax.random.normal(rng, dims, jnp.float32) * deviation * gain
    return jnp.minimum(jnp.maximum(values, -bound), bound).astype(kind)


def setup_inputs(seed: int = 0) -> dict:
    seeds = jax.random.split(jax.random.key(seed), 7)
    return {
        "tokens": noise(seeds[0], (TOKENS, D), 1.0, 6.0, ((0, 16), (1, 2))),
        "grad_out": noise(seeds[1], (TOKENS, D), 1.0, 6.0, ((0, 16), (1, 2))),
        "expert_ids": draw_expert_ids(jax.random.fold_in(seeds[6], 71), 0),
        "gate_score": noise(seeds[3], (TOKENS, TOPK), 1.5, 6.0, (), jnp.float32),
        "w_gate_up": noise(seeds[4], (EXPERTS, D, 2, H), D ** -0.5, 0.078125, ((0, 16), (1, 2))),
        "w_down": noise(seeds[5], (EXPERTS, H, D), H ** -0.5, 0.1875, ((0, 16), (2, 2))),
    }


def route_weights(gate_score):
    sigmoid_score = jax.nn.sigmoid(gate_score)
    return 2.5 * sigmoid_score / jnp.sum(sigmoid_score, axis=1, keepdims=True)


def reference(tokens, grad_out, expert_ids, gate_score, w_gate_up, w_down):
    weights = route_weights(gate_score)
    most_rows = N_EXPERT * CAP
    flat_gate_up = w_gate_up.reshape(EXPERTS, D, 2 * H)

    def per_expert(totals, stacked):
        acc_out, acc_grad = totals
        number, gate_up, down_proj = stacked
        names_it = expert_ids == number
        hits = jnp.sum(names_it.astype(jnp.int32), axis=1)
        row_order = jnp.argsort(1 - hits, stable=True)[:most_rows]
        is_valid = hits[row_order].astype(jnp.float32)
        route_share = jnp.sum(jnp.where(names_it, weights, 0.0), axis=1)[row_order]
        picked_rows = tokens[row_order]
        gate_both = jnp.dot(picked_rows, gate_up, preferred_element_type=jnp.float32)
        gate_pre = gate_both[:, :H]
        up_pre = gate_both[:, H:]
        hidden = (jax.nn.silu(gate_pre) * up_pre).astype(jnp.bfloat16)
        expert_out = jnp.dot(hidden, down_proj, preferred_element_type=jnp.float32).astype(jnp.bfloat16)
        cotangent = grad_out[row_order]
        hidden_grad = jnp.dot(cotangent, down_proj.T, preferred_element_type=jnp.float32) * route_share[:, None]
        sigmoid_gate = jax.nn.sigmoid(gate_pre)
        gate_grad = hidden_grad * up_pre * sigmoid_gate * (1.0 + gate_pre * (1.0 - sigmoid_gate))
        up_grad = hidden_grad * gate_pre * sigmoid_gate
        pre_grad = jnp.concatenate([gate_grad, up_grad], axis=1).astype(jnp.bfloat16)
        input_grad = jnp.dot(pre_grad, gate_up.T, preferred_element_type=jnp.float32).astype(jnp.bfloat16)
        group_of = number // N_EXPERT
        acc_out = acc_out.at[row_order, group_of].add(expert_out.astype(jnp.float32) * (route_share * is_valid)[:, None])
        acc_grad = acc_grad.at[row_order, group_of].add(input_grad.astype(jnp.float32) * is_valid[:, None])
        return (acc_out, acc_grad), None

    empty_sum = jnp.zeros((TOKENS, N_GROUP, D), jnp.float32)
    numbers = jnp.arange(EXPERTS, dtype=jnp.int32)
    (acc_out, acc_grad), _ = lax.scan(per_expert, (empty_sum, empty_sum), (numbers, flat_gate_up, w_down))
    group_out = lax.optimization_barrier(acc_out.astype(jnp.bfloat16))
    group_grad = lax.optimization_barrier(acc_grad.astype(jnp.bfloat16))
    layer_out = jnp.sum(group_out.astype(jnp.float32), axis=1).astype(jnp.bfloat16)
    grad_in = jnp.sum(group_grad.astype(jnp.float32), axis=1).astype(jnp.bfloat16)
    return layer_out, grad_in
```

```python
import functools

import jax
import jax.numpy as jnp
from jax import lax
from jax.experimental import pallas as pl
from jax.experimental.pallas import tpu as pltpu
from jax.sharding import PartitionSpec as P

HIGHEST = lax.Precision.HIGHEST


def route_weights(gate_score):
    sigmoid_score = jax.nn.sigmoid(gate_score)
    return 2.5 * sigmoid_score / jnp.sum(sigmoid_score, axis=1, keepdims=True)


def slot_matrix(marked, places):
    count = marked.shape[-2]
    order = jnp.arange(count, dtype=jnp.int32)
    earlier = (order[:, None] >= order[None, :]).astype(jnp.bfloat16)
    running = jnp.einsum(
        "ij,...jk->...ik",
        earlier,
        marked.astype(jnp.bfloat16),
        preferred_element_type=jnp.float32,
    )
    slot_range = jnp.arange(1, places + 1, dtype=jnp.int32).astype(jnp.float32)
    matched = marked[..., None] & (running[..., None] == slot_range)
    return jnp.moveaxis(matched, -3, -1).astype(jnp.float32)


def local_grad(gate_pre, up_pre, hidden_grad):
    sigmoid_gate = jax.nn.sigmoid(gate_pre)
    gate_grad = hidden_grad * up_pre * sigmoid_gate * (1.0 + gate_pre * (1.0 - sigmoid_gate))
    up_grad = hidden_grad * gate_pre * sigmoid_gate
    return jnp.stack([gate_grad, up_grad], axis=1).astype(jnp.bfloat16)


def across(blocks):
    return lax.all_to_all(blocks, "group", split_axis=0, concat_axis=0, tiled=True)


def within(blocks):
    return lax.all_to_all(blocks, "expert", split_axis=0, concat_axis=0, tiled=True)


def share_sum(partial_value):
    return lax.psum_scatter(partial_value, "dp", scatter_dimension=2, tiled=True)


def share_fold(shares, step_fn, start_value):
    return step_fn(start_value, lax.all_gather(shares, "dp", axis=2, tiled=True), jnp.int32(0))


MESH = pl.DeviceIdType.MESH
LANES = 2
TILE = 256
STRIP = 16
HALVES = 2
LINES = 4
SCHEDULE = (
    ("gather", 0, 0, 0),
    ("separate", 0),
    ("gather", 0, 0, 1),
    ("gather", 1, 0, 1),
    ("separate", 1),
    ("gather", 0, 1, 0),
    ("separate", 2),
    ("separate", 3),
    ("gather", 0, 1, 1),
    ("gather", 0, 2, 1),
    ("gather", 1, 0, 0),
    ("separate", 4),
    ("gather", 1, 1, 1),
    ("multiply_in", 0, 0),
    ("gather", 0, 2, 0),
    ("multiply_in", 0, 1),
    ("gather", 0, 3, 0),
    ("gather", 0, 3, 1),
    ("gather", 1, 1, 0),
    ("gather", 1, 2, 0),
    ("gather", 1, 3, 1),
    ("multiply_in", 1, 0),
    ("gather", 1, 3, 0),
    ("activate_out", 0),
    ("multiply_out", 0, 0),
    ("multiply_in", 1, 1),
    ("multiply_out", 0, 1),
    ("multiply_grad", 0),
    ("gather", 1, 2, 1),
    ("give_back", 0, 1, 1),
    ("give_back", 0, 1, 0),
    ("activate_out", 1),
    ("multiply_out", 1, 0),
    ("multiply_grad", 1),
    ("multiply_out", 1, 1),
    ("give_back", 0, 3, 0),
    ("activate_back", 0),
    ("give_back", 0, 2, 0),
    ("multiply_back", 0, 0),
    ("give_back", 0, 3, 1),
    ("multiply_back", 0, 1),
    ("give_back", 0, 2, 1),
    ("activate_back", 1),
    ("give_back", 1, 1, 0),
    ("multiply_back", 1, 0),
    ("finish", 0, 0),
    ("give_back", 1, 1, 1),
    ("multiply_back", 1, 1),
    ("give_back", 1, 3, 0),
    ("give_back", 1, 2, 0),
    ("give_back", 1, 3, 1),
    ("give_back", 1, 2, 1),
    ("finish", 0, 1),
    ("finish", 1, 0),
    ("finish", 1, 1),
)


def visit_order(lines):
    orders = []
    for line in range(lines):
        orders.append(sorted(range(lines), key=lambda level: (abs(level - line), level)))
    for line in range(lines // 2, lines):
        orders[line] = [lines - 1 - level for level in orders[lines - 1 - line]]
    return orders


def layer_kernel(
    tokens, grad_out, ids, scores, gate_hbm, down_hbm,
    layer_out, grad_in,
    stage, weights, down, leaving, rows, own_pre, own_grad, out_pre, out_grad, in_pre, in_grad,
    hidden, pre, parts, side, land, passing, leaving_core, home, share, place_table,
    stage_sem, down_sem, pair_send, pair_recv, row_send, row_recv,
    pre_send, pre_recv, grad_send, grad_recv,
    side_send, side_recv, land_send, land_recv, core_send, core_recv,
):
    my_group = lax.axis_index("group")
    me = lax.axis_index("expert")
    my_share = lax.axis_index("dp")
    other = 1 - my_group
    line, lane = me // LANES, lax.rem(me, LANES)
    other_lane = 1 - lane
    beside = line * LANES + other_lane
    _, groups, visitors, features = leaving.shape
    per_column = tokens.shape[0]
    token_count = ids.shape[1]
    lines = side.shape[2]
    members = lines * LANES
    hidden_size = down.shape[0]
    half_lines = lines // HALVES
    half_members = half_lines * LANES
    block_rows = groups * visitors
    half_rows = half_members * block_rows
    half_features = features // HALVES
    my_half = line // half_lines
    orders = visit_order(lines)
    chunks = stage_sem.shape[0]

    def level_at(step):
        return sum(
            (line == place).astype(jnp.int32) * orders[place][step] for place in range(lines)
        )

    def remote(src, dst, send, recv, where):
        return pltpu.make_async_remote_copy(
            src_ref=src, dst_ref=dst, send_sem=send, recv_sem=recv,
            device_id=where, device_id_type=MESH,
        )

    chunk_rows = stage.shape[0] // chunks
    stage_copies = []
    for chunk in range(chunks):
        span = pl.ds(chunk * chunk_rows, chunk_rows)
        stage_copies.append(
            pltpu.make_async_copy(gate_hbm.at[span], stage.at[span], stage_sem.at[chunk])
        )
    down_copy = pltpu.make_async_copy(down_hbm, down, down_sem)

    barrier = pltpu.get_barrier_semaphore()

    def hello(where):
        pl.semaphore_signal(barrier, inc=1, device_id=where, device_id_type=MESH)

    hello({"group": other})
    hello({"expert": beside})
    hello({"dp": 1 - my_share})
    for step in range(1, lines):
        hello({"expert": level_at(step) * LANES + lane})
    for copy in stage_copies:
        copy.start()
    down_copy.start()

    def wide(value):
        return value.astype(jnp.float32)

    def half_dot(left, right):
        return jnp.dot(
            left.astype(jnp.bfloat16), right.astype(jnp.bfloat16),
            preferred_element_type=jnp.float32,
        )

    grouped = wide((ids[0:1, :] >= members).astype(jnp.int32))

    def token_iota(dimension):
        return lax.broadcasted_iota(jnp.int32, (token_count, token_count), dimension)

    before, after = token_iota(0), token_iota(1)
    together = jnp.logical_and(before // per_column == after // per_column, before < after)
    ranked = half_dot(
        jnp.concatenate([1.0 - grouped, grouped], axis=0), wide(together.astype(jnp.int32))
    )
    slot = jnp.where(grouped > 0.5, visitors + ranked[1:2], ranked[0:1])
    first_token = (my_group * members + me) * per_column
    token_of = lax.broadcasted_iota(jnp.int32, (token_count, per_column), 0)
    column_of = lax.broadcasted_iota(jnp.int32, (token_count, per_column), 1)
    own_slot = half_dot(slot, wide((token_of == first_token + column_of).astype(jnp.int32)))
    row_of = lax.broadcasted_iota(jnp.int32, (block_rows, per_column), 0)
    place_table[...] = wide((wide(row_of) == own_slot).astype(jnp.int32)).astype(jnp.bfloat16)
    for array, values in enumerate((tokens, grad_out)):
        moved = jnp.dot(
            place_table[...], values[...], preferred_element_type=jnp.float32
        ).astype(jnp.bfloat16)
        for group in range(groups):
            leaving[array, group] = moved[group * visitors:(group + 1) * visitors]
        rows[array, me, my_group] = leaving[array, my_group]

    pl.semaphore_wait(barrier, 3 + lines - 1)

    def pair_copy(array):
        return remote(
            leaving.at[array, other], rows.at[array, me, my_group],
            pair_send.at[array], pair_recv.at[array], {"group": other},
        )

    def pair_wait(array):
        remote(
            leaving.at[array, my_group], rows.at[array, me, other],
            pair_send.at[array], pair_recv.at[array], {"group": other},
        ).wait_recv()

    def hop(way, array, block, piece, target):
        where = rows.at[array, block, piece]
        return remote(
            where, where, row_send.at[way, array, block, piece],
            row_recv.at[array, block, piece], {"expert": target},
        )

    def hop_side(array, block, piece):
        return hop(0, array, block, piece, beside)

    has_up = line < lines - 1
    has_down = line > 0

    def forward(act, array, step, piece):
        level = level_at(step)
        block = level * LANES + lane
        pl.when(jnp.logical_and(level <= line, has_up))(
            lambda: act(hop(1, array, block, piece, me + LANES))
        )
        pl.when(jnp.logical_and(level >= line, has_down))(
            lambda: act(hop(2, array, block, piece, me - LANES))
        )
        act(hop_side(array, block, piece))

    def piece_at(index):
        return my_group if index == 0 else other

    def begin(copy):
        copy.start()

    def sent(copy):
        copy.wait_send()

    def gather(array, step, index):
        piece = piece_at(index)
        mine = level_at(step) * LANES + lane
        if step == 0:
            if index == 1:
                pair_wait(array)
        else:
            hop_side(array, mine, piece).wait_recv()
        forward(begin, array, step, piece)

    def gathered(array, stage_index):
        for step in range(stage_index * half_lines, (stage_index + 1) * half_lines):
            theirs = level_at(step) * LANES + other_lane
            for index in range(groups):
                hop_side(array, theirs, piece_at(index)).wait_recv()

    span_rows = STRIP * 2 * (hidden_size // 128)

    def separate(chunk):
        stage_copies[chunk].wait()
        to = lax.broadcasted_iota(jnp.int32, (span_rows, span_rows), 0)
        source = lax.broadcasted_iota(jnp.int32, (span_rows, span_rows), 1)
        per_row = span_rows // STRIP
        select = (source == lax.rem(to, STRIP) * per_row + to // STRIP).astype(jnp.bfloat16)
        passes = chunk_rows // (2 * span_rows)
        unroll = next(count for count in (8, 4, 2, 1) if passes % count == 0)

        def one(index, carry):
            at = chunk * passes + index
            first = pl.multiple_of(at * 2 * span_rows, 2 * span_rows)
            both = jnp.concatenate(
                [stage[pl.ds(first, span_rows)], stage[pl.ds(first + span_rows, span_rows)]],
                axis=1,
            )
            moved = jnp.dot(select, both, preferred_element_type=jnp.float32).astype(jnp.bfloat16)
            base = pl.multiple_of(at * 2 * STRIP, 2 * STRIP)
            for slot_at in range(per_row):
                column = (slot_at % 2) * hidden_size + (slot_at // 2) * 128
                for half in range(2):
                    weights[pl.ds(base + half * STRIP, STRIP), column:column + 128] = moved[
                        slot_at * STRIP:(slot_at + 1) * STRIP, half * 128:(half + 1) * 128
                    ]
            return carry

        lax.fori_loop(0, passes, one, 0, unroll=unroll)

    def half_at(stage_index):
        return my_half if stage_index == 0 else 1 - my_half

    def half_block(array, half):
        found = rows[array, pl.ds(half * half_members, half_members)]
        return found.reshape(half_rows, features)

    def tile_at(index):
        return pl.ds(pl.multiple_of(index * TILE, TILE), TILE)

    def pre_copy(stage_index, kind):
        columns = pl.ds(kind * hidden_size, hidden_size)
        return remote(
            out_pre.at[stage_index, :, columns], in_pre.at[stage_index, :, columns],
            pre_send.at[stage_index, kind], pre_recv.at[stage_index, kind],
            {"dp": 1 - my_share},
        )

    def grad_copy(stage_index):
        return remote(
            out_grad.at[stage_index], in_grad.at[stage_index],
            grad_send.at[stage_index], grad_recv.at[stage_index], {"dp": 1 - my_share},
        )

    def multiply_in(stage_index, kind):
        if kind == 0:
            gathered(0, stage_index)
        columns = pl.ds(kind * hidden_size, hidden_size)
        value = jnp.dot(
            half_block(0, half_at(stage_index)), weights[:, columns],
            preferred_element_type=jnp.float32,
        )
        own_pre[stage_index, :, columns] = value
        out_pre[stage_index, :, columns] = value.astype(jnp.bfloat16)
        pre_copy(stage_index, kind).start()

    def down_ready(stage_index):
        if stage_index == 0 and not waited:
            waited.append(True)
            down_copy.wait()

    waited = []

    def multiply_grad(stage_index):
        gathered(1, stage_index)
        down_ready(stage_index)
        value = lax.dot_general(
            half_block(1, half_at(stage_index)), down[...], (((1,), (1,)), ((), ())),
            preferred_element_type=jnp.float32,
        )
        own_grad[stage_index] = value
        out_grad[stage_index] = value.astype(jnp.bfloat16)
        grad_copy(stage_index).start()

    def make_share():
        score = jax.nn.sigmoid(scores[...])
        weight = 2.5 * score / jnp.sum(score, axis=0, keepdims=True)
        my_expert = my_group * members + me
        mine = jnp.sum(jnp.where(ids[...] == my_expert, weight, 0.0), axis=0, keepdims=True)
        token = lax.broadcasted_iota(jnp.int32, (1, token_count), 1)
        member = lax.rem(token // per_column, members)
        source = token // (per_column * members)
        rank = jnp.where(grouped > 0.5, ranked[1:2], ranked[0:1])
        row = wide(member * block_rows + source * visitors) + rank
        here = grouped == wide(my_group + jnp.zeros((1, token_count), jnp.int32))
        row = jnp.where(here, row, -1.0)
        at = wide(lax.broadcasted_iota(jnp.int32, (HALVES * half_rows, token_count), 0))
        share[...] = jnp.sum(jnp.where(at == row, mine, 0.0), axis=1, keepdims=True)

    def half_share(stage_index):
        first = pl.multiple_of(half_at(stage_index) * half_rows, half_rows)
        return share[pl.ds(first, half_rows), :]

    def put_parts(array, cut, stage_index, value):
        half = half_at(stage_index)
        parts[array, cut, pl.ds(half * half_members, half_members)] = value.astype(
            jnp.bfloat16
        ).reshape(half_members, block_rows, half_features)
        for step in range((stage_index + 1) * half_lines - 1, stage_index * half_lines - 1, -1):
            side_copy(array, step, cut).start()

    def activate_out(stage_index):
        if stage_index == 0:
            make_share()
        for kind in range(2):
            pre_copy(stage_index, kind).wait_recv()
        weight = half_share(stage_index)

        def one(index, carry):
            columns = tile_at(index)
            up_columns = tile_at(index + hidden_size // TILE)
            gate_pre = own_pre[stage_index, :, columns] + wide(in_pre[stage_index, :, columns])
            up_pre = own_pre[stage_index, :, up_columns] + wide(
                in_pre[stage_index, :, up_columns]
            )
            gate_sigmoid = jax.nn.sigmoid(gate_pre)
            gate_silu = gate_pre * gate_sigmoid
            hidden[:, columns] = (gate_silu * up_pre).astype(jnp.bfloat16)
            own_pre[stage_index, :, columns] = (
                weight * up_pre * gate_sigmoid * (1.0 + gate_pre * (1.0 - gate_sigmoid))
            )
            own_pre[stage_index, :, up_columns] = weight * gate_silu
            return carry

        lax.fori_loop(0, hidden_size // TILE, one, 0)

    def multiply_out(stage_index, cut):
        down_ready(stage_index)
        value = jnp.dot(
            hidden[...], down[:, cut * half_features:(cut + 1) * half_features],
            preferred_element_type=jnp.float32,
        )
        put_parts(0, cut, stage_index, value * half_share(stage_index))

    def activate_back(stage_index):
        grad_copy(stage_index).wait_recv()

        def one(index, carry):
            columns = tile_at(index)
            up_columns = tile_at(index + hidden_size // TILE)
            grad = own_grad[stage_index, :, columns] + wide(in_grad[stage_index, :, columns])
            pre[:, columns] = (grad * own_pre[stage_index, :, columns]).astype(jnp.bfloat16)
            pre[:, up_columns] = (grad * own_pre[stage_index, :, up_columns]).astype(
                jnp.bfloat16
            )
            return carry

        lax.fori_loop(0, hidden_size // TILE, one, 0)

    def multiply_back(stage_index, cut):
        value = lax.dot_general(
            pre[...], weights[cut * half_features:(cut + 1) * half_features, :],
            (((1,), (1,)), ((), ())), preferred_element_type=jnp.float32,
        )
        put_parts(1, cut, stage_index, value)

    def side_copy(array, step, cut):
        level = level_at(step)
        return remote(
            parts.at[array, cut, level * LANES + other_lane], side.at[array, cut, level],
            side_send.at[array, cut, level], side_recv.at[array, cut, level],
            {"expert": beside},
        )

    def land_copy(array, step, cut):
        return remote(
            passing.at[array, cut, step - 1], land.at[array, cut, line],
            land_send.at[array, cut, step - 1], land_recv.at[array, cut, line],
            {"expert": level_at(step) * LANES + lane},
        )

    def land_wait(array, step, cut):
        source = level_at(step)
        remote(
            passing.at[array, cut, step - 1], land.at[array, cut, source],
            land_send.at[array, cut, step - 1], land_recv.at[array, cut, source],
            {"expert": source * LANES + lane},
        ).wait_recv()

    def pair_sum(array, step, cut):
        side_copy(array, step, cut).wait_recv()
        level = level_at(step)
        return wide(parts[array, cut, level * LANES + lane]) + wide(side[array, cut, level])

    def give_back(array, step, cut):
        passing[array, cut, step - 1] = pair_sum(array, step, cut).astype(jnp.bfloat16)
        land_copy(array, step, cut).start()

    def cut_columns(cut):
        return pl.ds(cut * half_features, half_features)

    def core_copy(array, cut):
        return remote(
            leaving_core.at[array, cut, pl.ds(other * visitors, visitors)],
            home.at[array, my_group, :, cut_columns(cut)],
            core_send.at[array, cut], core_recv.at[array, cut], {"group": other},
        )

    def core_wait(array, cut):
        remote(
            leaving_core.at[array, cut, pl.ds(my_group * visitors, visitors)],
            home.at[array, other, :, cut_columns(cut)],
            core_send.at[array, cut], core_recv.at[array, cut], {"group": other},
        ).wait_recv()

    def finish(array, cut):
        total = pair_sum(array, 0, cut)
        for step in range(1, lines):
            land_wait(array, step, cut)
            total = total + wide(land[array, cut, level_at(step)])
        leaving_core[array, cut] = total.astype(jnp.bfloat16)
        core_copy(array, cut).start()
        home[array, my_group, :, cut_columns(cut)] = leaving_core[
            array, cut, pl.ds(my_group * visitors, visitors)
        ]

    def put_home(array, cut, result):
        core_wait(array, cut)
        found = home[array, :, :, cut_columns(cut)].reshape(block_rows, half_features)
        result[:, cut_columns(cut)] = lax.dot_general(
            place_table[...], found, (((0,), (0,)), ((), ())),
            preferred_element_type=jnp.float32,
        ).astype(jnp.bfloat16)

    for array in range(2):
        pair_copy(array).start()

    events = dict(
        gather=gather, separate=separate, multiply_in=multiply_in, multiply_grad=multiply_grad,
        activate_out=activate_out, activate_back=activate_back, multiply_out=multiply_out,
        multiply_back=multiply_back, give_back=give_back, finish=finish,
    )
    for name, *where in SCHEDULE:
        events[name](*where)

    for array, result in enumerate((layer_out, grad_in)):
        for cut in range(HALVES):
            put_home(array, cut, result)
    for array in range(2):
        pair_copy(array).wait_send()
        for step in range(lines):
            for index in range(groups):
                forward(sent, array, step, piece_at(index))
        for cut in range(HALVES):
            core_copy(array, cut).wait_send()
            for step in range(lines):
                side_copy(array, step, cut).wait_send()
            for step in range(1, lines):
                land_copy(array, step, cut).wait_send()
    for stage_index in range(HALVES):
        for kind in range(2):
            pre_copy(stage_index, kind).wait_send()
        grad_copy(stage_index).wait_send()


def dense_device(tokens, grad_out, expert_ids, gate_score, w_gate_up, w_down):
    groups = lax.axis_size("group")
    members = lax.axis_size("expert")
    per_column, features = tokens.shape
    hidden_size = w_gate_up.shape[3]
    lane_blocks = hidden_size // 128
    gate_rows = jnp.transpose(
        w_gate_up[0].reshape(features, 2, lane_blocks, 128), (0, 2, 1, 3)
    ).reshape(features * lane_blocks * 2, 128)
    down_weights = w_down[0]
    visitors = per_column // groups
    lines = members // LANES
    half_rows = members * per_column // HALVES
    half, full = jnp.bfloat16, jnp.float32
    passes = features // (2 * STRIP)
    chunks = 5 if passes % 5 == 0 else 1
    dma = pltpu.SemaphoreType.DMA
    piece = (groups, visitors, features)
    block = (per_column, features // HALVES)
    vmem = pl.BlockSpec(memory_space=pltpu.VMEM)
    anywhere = pl.BlockSpec(memory_space=pl.ANY)
    result = jax.ShapeDtypeStruct(tokens.shape, tokens.dtype)
    return pl.pallas_call(
        layer_kernel,
        out_shape=(result, result),
        in_specs=[vmem, vmem, vmem, vmem, anywhere, anywhere],
        out_specs=(vmem, vmem),
        scratch_shapes=[
            pltpu.VMEM(gate_rows.shape, half),
            pltpu.VMEM((features, 2 * hidden_size), half),
            pltpu.VMEM(down_weights.shape, half),
            pltpu.VMEM((2, *piece), half),
            pltpu.VMEM((2, members, *piece), half),
            pltpu.VMEM((HALVES, half_rows, 2 * hidden_size), full),
            pltpu.VMEM((HALVES, half_rows, hidden_size), full),
            pltpu.VMEM((HALVES, half_rows, 2 * hidden_size), half),
            pltpu.VMEM((HALVES, half_rows, hidden_size), half),
            pltpu.VMEM((HALVES, half_rows, 2 * hidden_size), half),
            pltpu.VMEM((HALVES, half_rows, hidden_size), half),
            pltpu.VMEM((half_rows, hidden_size), half),
            pltpu.VMEM((half_rows, 2 * hidden_size), half),
            pltpu.VMEM((2, HALVES, members, *block), half),
            pltpu.VMEM((2, HALVES, lines, *block), half),
            pltpu.VMEM((2, HALVES, lines, *block), half),
            pltpu.VMEM((2, HALVES, lines - 1, *block), half),
            pltpu.VMEM((2, HALVES, *block), half),
            pltpu.VMEM((2, *piece), half),
            pltpu.VMEM((members * per_column, 1), full),
            pltpu.VMEM((per_column, per_column), half),
            dma((chunks,)), dma(()), dma((2,)), dma((2,)),
            dma((3, 2, members, groups)), dma((2, members, groups)),
            dma((HALVES, 2)), dma((HALVES, 2)), dma((HALVES,)), dma((HALVES,)),
            dma((2, HALVES, lines)), dma((2, HALVES, lines)),
            dma((2, HALVES, lines - 1)), dma((2, HALVES, lines)),
            dma((2, HALVES)), dma((2, HALVES)),
        ],
        compiler_params=pltpu.CompilerParams(
            collective_id=0, has_side_effects=True, vmem_limit_bytes=58 << 20
        ),
        name="layer",
    )(
        tokens, grad_out, jnp.transpose(expert_ids), jnp.transpose(gate_score),
        gate_rows, down_weights,
    )


def on_device(tokens, grad_out, expert_ids, gate_score, w_gate_up, w_down):
    groups = lax.axis_size("group")
    members = lax.axis_size("expert")
    my_group = lax.axis_index("group")
    my_index = lax.axis_index("expert")
    per_column = tokens.shape[0]
    features = tokens.shape[1]
    visitors = per_column // 2
    top_count = expert_ids.shape[1]
    arrivals = groups * visitors
    capacity = min(arrivals, (3 * per_column * top_count + 2 * members - 1) // (2 * members))
    expert_rows = members * capacity
    weights = route_weights(gate_score).reshape(groups, members, per_column, top_count)
    pick_ids = expert_ids.reshape(groups, members, per_column, top_count)
    group_range = jnp.arange(groups, dtype=jnp.int32)
    my_picks = pick_ids[my_group, my_index]
    visits_mine = jnp.any(my_picks[:, :, None] // members == group_range, axis=1)
    leave_table = slot_matrix(visits_mine, visitors).astype(jnp.bfloat16)
    visits_here = jnp.any(pick_ids // members == my_group, axis=3)
    arrival_table = slot_matrix(visits_here[..., None], visitors)[:, :, 0]
    row_ids = jnp.einsum(
        "gest,getk->gesk", arrival_table, pick_ids.astype(jnp.float32), precision=HIGHEST
    )
    row_weights = jnp.einsum("gest,getk->gesk", arrival_table, weights, precision=HIGHEST)
    targets = (my_group * members + jnp.arange(members, dtype=jnp.int32)).astype(jnp.float32)
    matched = row_ids[..., None] == targets
    picked = jnp.any(matched, axis=3)
    picked_weight = jnp.sum(jnp.where(matched, row_weights[..., None], 0.0), axis=3)
    send_flags = picked[:, my_index].reshape(arrivals, members)
    send_table = slot_matrix(send_flags, capacity)
    send_share = jnp.transpose(picked_weight[:, my_index].reshape(arrivals, members))
    send_weight = send_table * send_share[:, None, :]
    came_flags = jnp.transpose(picked[:, :, :, my_index], (1, 0, 2)).reshape(members, arrivals)
    came_table = slot_matrix(came_flags[..., None], capacity)[:, 0]
    came_share = jnp.transpose(picked_weight[:, :, :, my_index], (1, 0, 2)).reshape(
        members, arrivals
    )
    slot_weight = jnp.einsum("ecr,er->ec", came_table, came_share, precision=HIGHEST).reshape(
        expert_rows
    )

    def dispatch(values):
        leaving = jnp.einsum(
            "gst,tf->gsf", leave_table, values, preferred_element_type=jnp.float32
        ).astype(jnp.bfloat16)
        arrived = across(leaving).reshape(arrivals, features)
        onward = jnp.einsum(
            "ecr,rf->ecf",
            send_table.astype(jnp.bfloat16),
            arrived,
            preferred_element_type=jnp.float32,
        ).astype(jnp.bfloat16)
        return within(onward).reshape(expert_rows, features)

    def combine(values, table):
        returned = within(values.reshape(members, capacity, features)).astype(jnp.float32)
        summed = jnp.einsum("ecr,ecf->rf", table, returned, precision=HIGHEST).astype(jnp.bfloat16)
        home = across(summed.reshape(groups, visitors, features))
        return jnp.einsum(
            "gst,gsf->tf", leave_table, home, preferred_element_type=jnp.float32
        ).astype(jnp.bfloat16)

    rows_in = dispatch(tokens)
    rows_grad = dispatch(grad_out)
    gate_weights = w_gate_up[0]
    down_weights = w_down[0]
    partial_value = jnp.einsum(
        "rf,fkh->rkh", rows_in, gate_weights, preferred_element_type=jnp.float32
    )
    grad_partial = jnp.einsum(
        "rf,hf->rh", rows_grad, down_weights, preferred_element_type=jnp.float32
    )
    empty_rows = jnp.zeros((expert_rows, features), jnp.float32)
    gate_both = share_sum(partial_value)
    gate_pre = gate_both[:, 0]
    up_pre = gate_both[:, 1]
    hidden = (jax.nn.silu(gate_pre) * up_pre).astype(jnp.bfloat16)[:, None, :]

    def down_step(running_sum, gathered, first_row):
        return jnp.dot(gathered[:, 0], down_weights, preferred_element_type=jnp.float32)

    expert_out = share_fold(hidden, down_step, empty_rows).astype(jnp.bfloat16)
    hidden_grad = share_sum(grad_partial[:, None, :])[:, 0] * slot_weight[:, None]
    pre_grad = local_grad(gate_pre, up_pre, hidden_grad)

    def input_step(running_sum, gathered, first_row):
        return jnp.einsum("rkh,fkh->rf", gathered, gate_weights, preferred_element_type=jnp.float32)

    expert_grad = share_fold(pre_grad, input_step, empty_rows).astype(jnp.bfloat16)
    layer_out = combine(expert_out, send_weight)
    grad_in = combine(expert_grad, send_table)
    return (layer_out, grad_in)


def per_device(tokens, grad_out, expert_ids, gate_score, w_gate_up, w_down):
    members = lax.axis_size("expert")
    dense = (
        expert_ids.shape[1] == members
        and members == LINES * LANES
        and lax.axis_size("group") == 2
        and lax.axis_size("dp") == 2
        and tokens.shape[0] == 2 * STRIP
        and tokens.shape[1] % (2 * TILE) == 0
        and w_gate_up.shape[3] % TILE == 0
    )
    plan = dense_device if dense else on_device
    return plan(tokens, grad_out, expert_ids, gate_score, w_gate_up, w_down)


def solution(mesh):
    return jax.shard_map(
        per_device,
        mesh=mesh,
        in_specs=(
            P(("group", "expert"), "dp"),
            P(("group", "expert"), "dp"),
            P(),
            P(),
            P(("group", "expert"), "dp", None, None),
            P(("group", "expert"), None, "dp"),
        ),
        out_specs=(P(("group", "expert"), "dp"), P(("group", "expert"), "dp")),
        check_vma=False,
    )
```

```python
import functools

import jax
import jax.numpy as jnp
from jax import lax
from jax.experimental import pallas as pl
from jax.experimental.pallas import tpu as pltpu
from jax.sharding import PartitionSpec as P

HIGHEST = lax.Precision.HIGHEST


def route_weights(gate_score):
    sigmoid_score = jax.nn.sigmoid(gate_score)
    return 2.5 * sigmoid_score / jnp.sum(sigmoid_score, axis=1, keepdims=True)


def slot_matrix(marked, places):
    count = marked.shape[-2]
    order = jnp.arange(count, dtype=jnp.int32)
    earlier = (order[:, None] >= order[None, :]).astype(jnp.bfloat16)
    running = jnp.einsum(
        "ij,...jk->...ik",
        earlier,
        marked.astype(jnp.bfloat16),
        preferred_element_type=jnp.float32,
    )
    slot_range = jnp.arange(1, places + 1, dtype=jnp.int32).astype(jnp.float32)
    matched = marked[..., None] & (running[..., None] == slot_range)
    return jnp.moveaxis(matched, -3, -1).astype(jnp.float32)


def local_grad(gate_pre, up_pre, hidden_grad):
    sigmoid_gate = jax.nn.sigmoid(gate_pre)
    gate_grad = hidden_grad * up_pre * sigmoid_gate * (1.0 + gate_pre * (1.0 - sigmoid_gate))
    up_grad = hidden_grad * gate_pre * sigmoid_gate
    return jnp.stack([gate_grad, up_grad], axis=1).astype(jnp.bfloat16)


def across(blocks):
    return lax.all_to_all(blocks, "group", split_axis=0, concat_axis=0, tiled=True)


def within(blocks):
    return lax.all_to_all(blocks, "expert", split_axis=0, concat_axis=0, tiled=True)


def share_sum(partial_value):
    return lax.psum_scatter(partial_value, "dp", scatter_dimension=2, tiled=True)


def share_fold(shares, step_fn, start_value):
    return step_fn(start_value, lax.all_gather(shares, "dp", axis=2, tiled=True), jnp.int32(0))


MESH = pl.DeviceIdType.MESH
LANES = 2
TILE = 256
STRIP = 16
HALVES = 2
LINES = 4
SPAN = 128
BOTH_LANES = ((False, False), (False, True))
SCHEDULE = (
    ("gather", 0, 0, 0),
    ("separate", 0),
    ("separate", 1),
    ("gather", 0, 0, 1),
    ("separate", 2),
    ("gather", 1, 0, 1),
    ("separate", 3),
    ("gather", 0, 1, 0),
    ("separate", 4),
    ("multiply_level", 0, 0),
    ("gather", 0, 1, 1),
    ("gather", 0, 2, 1),
    ("multiply_level", 0, 1),
    ("gather", 0, 2, 0),
    ("gather", 1, 1, 1),
    ("gather", 0, 3, 0),
    ("multiply_level", 1, 0),
    ("gather", 0, 3, 1),
    ("gather", 1, 0, 0),
    ("multiply_level", 1, 1),
    ("gather", 1, 2, 0),
    ("gather_beside", 1, 0, 1),
    ("gather", 1, 1, 0),
    ("multiply_in", 1, 0),
    ("gather", 1, 2, 1),
    ("activate_out", 0),
    ("gather", 1, 3, 0),
    ("gather_beside", 1, 1, 1),
    ("multiply_in", 1, 1),
    ("gather", 1, 3, 1),
    ("multiply_out", 0, 0),
    ("multiply_out", 0, 1),
    ("gather_beside", 1, 2, 1),
    ("gather_beside", 1, 3, 1),
    ("multiply_grad", 1),
    ("activate_out", 1),
    ("multiply_out", 1, 0),
    ("give_back", 0, 1, 0),
    ("give_back", 0, 1, 1),
    ("multiply_grad", 0),
    ("multiply_out", 1, 1),
    ("give_back", 0, 3, 0),
    ("activate_back", 1),
    ("give_back", 0, 2, 0),
    ("multiply_back", 1, 0),
    ("give_back", 0, 3, 1),
    ("relay", 0, 3, 0),
    ("multiply_back", 1, 1),
    ("relay", 0, 2, 0),
    ("give_back", 0, 2, 1),
    ("give_back", 1, 3, 0),
    ("activate_back", 0),
    ("relay", 0, 3, 1),
    ("multiply_back", 0, 0),
    ("relay", 0, 2, 1),
    ("give_back", 1, 3, 1),
    ("relay", 1, 3, 0),
    ("give_back", 1, 2, 0),
    ("multiply_back", 0, 1),
    ("give_back", 1, 2, 1),
    ("give_back", 1, 1, 0),
    ("relay", 1, 3, 1),
    ("relay", 1, 2, 0),
    ("give_back", 1, 1, 1),
    ("relay", 1, 2, 1),
    ("finish", 0, 0),
    ("finish", 1, 0),
    ("finish", 0, 1),
    ("finish", 1, 1),
)


def visit_order(lines):
    orders = []
    for line in range(lines):
        orders.append(sorted(range(lines), key=lambda level: (abs(level - line), level)))
    for line in range(lines // 2, lines):
        orders[line] = [lines - 1 - level for level in orders[lines - 1 - line]]
    return orders


def layer_kernel(
    tokens, grad_out, ids, scores, gate_hbm, down_hbm,
    result,
    stage, weights, down, leaving, rows, own_pre, own_grad, out_pre, out_grad, in_pre, in_grad,
    hidden, pre, parts, side, land, relayed, passing, leaving_core, home, share, place_table,
    stage_sem, down_sem, pair_send, pair_recv, row_send, row_recv,
    level_send, level_recv, pre_send, pre_recv, grad_send, grad_recv,
    side_send, side_recv, land_send, land_recv, relay_recv, core_send, core_recv,
):
    my_group = lax.axis_index("group")
    me = lax.axis_index("expert")
    my_share = lax.axis_index("dp")
    other = 1 - my_group
    line, lane = me // LANES, lax.rem(me, LANES)
    other_lane = 1 - lane
    beside = line * LANES + other_lane
    _, groups, visitors, features = leaving.shape
    per_column = tokens.shape[0]
    token_count = ids.shape[1]
    lines = side.shape[2]
    members = lines * LANES
    hidden_size = down.shape[0]
    half_lines = lines // HALVES
    half_members = half_lines * LANES
    block_rows = groups * visitors
    half_rows = half_members * block_rows
    level_rows = LANES * block_rows
    half_features = features // HALVES
    my_half = line // half_lines
    orders = visit_order(lines)
    chunks = stage_sem.shape[0]

    def level_at(step):
        return sum(
            (line == place).astype(jnp.int32) * orders[place][step] for place in range(lines)
        )

    def remote(src, dst, send, recv, where):
        return pltpu.make_async_remote_copy(
            src_ref=src, dst_ref=dst, send_sem=send, recv_sem=recv,
            device_id=where, device_id_type=MESH,
        )

    chunk_rows = stage.shape[0] // chunks
    stage_copies = []
    for chunk in range(chunks):
        span = pl.ds(chunk * chunk_rows, chunk_rows)
        stage_copies.append(
            pltpu.make_async_copy(gate_hbm.at[span], stage.at[span], stage_sem.at[chunk])
        )
    down_copy = pltpu.make_async_copy(down_hbm, down, down_sem)

    barrier = pltpu.get_barrier_semaphore()

    def hello(where):
        pl.semaphore_signal(barrier, inc=1, device_id=where, device_id_type=MESH)

    hello({"group": other})
    hello({"expert": beside})
    hello({"dp": 1 - my_share})
    for step in range(1, lines):
        hello({"expert": level_at(step) * LANES + lane})
    for copy in stage_copies:
        copy.start()
    down_copy.start()

    def wide(value):
        return value.astype(jnp.float32)

    def half_dot(left, right):
        return jnp.dot(
            left.astype(jnp.bfloat16), right.astype(jnp.bfloat16),
            preferred_element_type=jnp.float32,
        )

    grouped = wide((ids[0:1, :] >= members).astype(jnp.int32))
    spans = token_count // SPAN
    folded = jnp.concatenate(
        [grouped[:, part * SPAN:(part + 1) * SPAN] for part in range(spans)], axis=0
    )

    def span_iota(shape, dimension):
        return lax.broadcasted_iota(jnp.int32, shape, dimension)

    before, after = span_iota((SPAN, SPAN), 0), span_iota((SPAN, SPAN), 1)
    together = jnp.logical_and(before // per_column == after // per_column, before < after)
    ranked = half_dot(
        jnp.concatenate([1.0 - folded, folded], axis=0), wide(together.astype(jnp.int32))
    )
    rank = jnp.where(folded > 0.5, ranked[spans:], ranked[:spans])
    first_token = (my_group * members + me) * per_column
    span_row = span_iota((spans, SPAN), 0)
    slots = jnp.where(span_row == first_token // SPAN, visitors * folded + rank, 0.0)
    slot = jnp.sum(slots, axis=0, keepdims=True)
    token_of = span_iota((SPAN, per_column), 0)
    column_of = span_iota((SPAN, per_column), 1)
    found_token = token_of == lax.rem(first_token, SPAN) + column_of
    own_slot = half_dot(slot, wide(found_token.astype(jnp.int32)))
    row_of = lax.broadcasted_iota(jnp.int32, (block_rows, per_column), 0)
    place_table[...] = wide((wide(row_of) == own_slot).astype(jnp.int32)).astype(jnp.bfloat16)
    for array, values in enumerate((tokens, grad_out)):
        moved = jnp.dot(
            place_table[...], values[...], preferred_element_type=jnp.float32
        ).astype(jnp.bfloat16)
        for group in range(groups):
            leaving[array, group] = moved[group * visitors:(group + 1) * visitors]
        rows[array, me, my_group] = leaving[array, my_group]

    pl.semaphore_wait(barrier, 3 + lines - 1)

    def pair_copy(array):
        return remote(
            leaving.at[array, other], rows.at[array, me, my_group],
            pair_send.at[array], pair_recv.at[array], {"group": other},
        )

    def pair_wait(array):
        remote(
            leaving.at[array, my_group], rows.at[array, me, other],
            pair_send.at[array], pair_recv.at[array], {"group": other},
        ).wait_recv()

    def hop(way, array, block, piece, target):
        where = rows.at[array, block, piece]
        return remote(
            where, where, row_send.at[way, array, block, piece],
            row_recv.at[array, block, piece], {"expert": target},
        )

    def hop_side(array, block, piece):
        return hop(0, array, block, piece, beside)

    has_up = line < lines - 1
    has_down = line > 0
    outer = jnp.logical_or(line == 0, line == lines - 1)

    def along(act, array, step, block, piece):
        level = level_at(step)
        pl.when(jnp.logical_and(level <= line, has_up))(
            lambda: act(hop(1, array, block, piece, me + LANES))
        )
        pl.when(jnp.logical_and(level >= line, has_down))(
            lambda: act(hop(2, array, block, piece, me - LANES))
        )

    def forward(act, array, step, index):
        piece = piece_at(index)
        block = level_at(step) * LANES + lane
        if step == 0:
            act(hop_side(array, block, piece))
        along(act, array, step, block, piece)
        if step and not BOTH_LANES[array][index]:
            act(hop_side(array, block, piece))

    def forward_beside(act, array, step, index):
        along(act, array, step, level_at(step) * LANES + other_lane, piece_at(index))

    def piece_at(index):
        return my_group if index == 0 else other

    def begin(copy):
        copy.start()

    def sent(copy):
        copy.wait_send()

    def gather(array, step, index):
        piece = piece_at(index)
        mine = level_at(step) * LANES + lane
        if step == 0:
            if index == 1:
                pair_wait(array)
        else:
            hop_side(array, mine, piece).wait_recv()
        forward(begin, array, step, index)

    def gather_beside(array, step, index):
        theirs = level_at(step) * LANES + other_lane
        hop_side(array, theirs, piece_at(index)).wait_recv()
        forward_beside(begin, array, step, index)

    def gathered_level(array, step):
        theirs = level_at(step) * LANES + other_lane
        for index in range(groups):
            if not BOTH_LANES[array][index]:
                hop_side(array, theirs, piece_at(index)).wait_recv()

    def gathered(array, stage_index):
        for step in range(stage_index * half_lines, (stage_index + 1) * half_lines):
            gathered_level(array, step)

    span_rows = STRIP * 2 * (hidden_size // 128)

    def separate(chunk):
        stage_copies[chunk].wait()
        to = lax.broadcasted_iota(jnp.int32, (span_rows, span_rows), 0)
        source = lax.broadcasted_iota(jnp.int32, (span_rows, span_rows), 1)
        per_row = span_rows // STRIP
        select = (source == lax.rem(to, STRIP) * per_row + to // STRIP).astype(jnp.bfloat16)
        passes = chunk_rows // (2 * span_rows)
        unroll = next(count for count in (8, 4, 2, 1) if passes % count == 0)

        def one(index, carry):
            at = chunk * passes + index
            first = pl.multiple_of(at * 2 * span_rows, 2 * span_rows)
            both = jnp.concatenate(
                [stage[pl.ds(first, span_rows)], stage[pl.ds(first + span_rows, span_rows)]],
                axis=1,
            )
            moved = jnp.dot(select, both, preferred_element_type=jnp.float32).astype(jnp.bfloat16)
            base = pl.multiple_of(at * 2 * STRIP, 2 * STRIP)
            for slot_at in range(per_row):
                column = (slot_at % 2) * hidden_size + (slot_at // 2) * 128
                for half in range(2):
                    weights[pl.ds(base + half * STRIP, STRIP), column:column + 128] = moved[
                        slot_at * STRIP:(slot_at + 1) * STRIP, half * 128:(half + 1) * 128
                    ]
            return carry

        lax.fori_loop(0, passes, one, 0, unroll=unroll)

    def half_at(stage_index):
        return my_half if stage_index == 0 else 1 - my_half

    def half_block(array, half):
        found = rows[array, pl.ds(half * half_members, half_members)]
        return found.reshape(half_rows, features)

    def tile_at(index):
        return pl.ds(pl.multiple_of(index * TILE, TILE), TILE)

    def pre_copy(stage_index, kind):
        columns = pl.ds(kind * hidden_size, hidden_size)
        return remote(
            out_pre.at[stage_index, :, columns], in_pre.at[stage_index, :, columns],
            pre_send.at[kind], pre_recv.at[kind],
            {"dp": 1 - my_share},
        )

    def grad_copy(stage_index):
        return remote(
            out_grad.at[stage_index], in_grad.at[stage_index],
            grad_send.at[stage_index], grad_recv.at[stage_index], {"dp": 1 - my_share},
        )

    def level_rows_of(step):
        first = lax.rem(level_at(step), half_lines) * level_rows
        return pl.ds(pl.multiple_of(first, level_rows), level_rows)

    def level_copy(step, kind):
        where = (0, level_rows_of(step), pl.ds(kind * hidden_size, hidden_size))
        return remote(
            out_pre.at[where], in_pre.at[where], level_send.at[step, kind],
            level_recv.at[step, kind], {"dp": 1 - my_share},
        )

    def multiply_level(step, kind):
        if kind == 0:
            gathered_level(0, step)
        columns = pl.ds(kind * hidden_size, hidden_size)
        found = rows[0, pl.ds(level_at(step) * LANES, LANES)].reshape(level_rows, features)
        value = jnp.dot(found, weights[:, columns], preferred_element_type=jnp.float32)
        own_pre[0, level_rows_of(step), columns] = value
        out_pre[0, level_rows_of(step), columns] = value.astype(jnp.bfloat16)
        level_copy(step, kind).start()

    def multiply_in(stage_index, kind):
        if kind == 0:
            gathered(0, stage_index)
        columns = pl.ds(kind * hidden_size, hidden_size)
        value = jnp.dot(
            half_block(0, half_at(stage_index)), weights[:, columns],
            preferred_element_type=jnp.float32,
        )
        own_pre[stage_index, :, columns] = value
        out_pre[stage_index, :, columns] = value.astype(jnp.bfloat16)
        pre_copy(stage_index, kind).start()

    def down_ready():
        if not waited:
            waited.append(True)
            down_copy.wait()

    waited = []

    def multiply_grad(stage_index):
        gathered(1, stage_index)
        down_ready()
        value = lax.dot_general(
            half_block(1, half_at(stage_index)), down[...], (((1,), (1,)), ((), ())),
            preferred_element_type=jnp.float32,
        )
        own_grad[stage_index] = value
        out_grad[stage_index] = value.astype(jnp.bfloat16)
        grad_copy(stage_index).start()

    def make_share():
        score = jax.nn.sigmoid(scores[...])
        weight = 2.5 * score / jnp.sum(score, axis=0, keepdims=True)
        my_expert = my_group * members + me
        mine = jnp.sum(jnp.where(ids[...] == my_expert, weight, 0.0), axis=0, keepdims=True)
        token = lax.broadcasted_iota(jnp.int32, (1, token_count), 1)
        member = lax.rem(token // per_column, members)
        source = token // (per_column * members)
        token_rank = jnp.concatenate([rank[part:part + 1] for part in range(spans)], axis=1)
        row = wide(member * block_rows + source * visitors) + token_rank
        here = grouped == wide(my_group + jnp.zeros((1, token_count), jnp.int32))
        row = jnp.where(here, row, -1.0)
        at = wide(lax.broadcasted_iota(jnp.int32, (HALVES * half_rows, token_count), 0))
        share[...] = jnp.sum(jnp.where(at == row, mine, 0.0), axis=1, keepdims=True)

    def half_share(stage_index):
        first = pl.multiple_of(half_at(stage_index) * half_rows, half_rows)
        return share[pl.ds(first, half_rows), :]

    def put_parts(array, cut, stage_index, value):
        half = half_at(stage_index)
        parts[array, cut, pl.ds(half * half_members, half_members)] = value.astype(
            jnp.bfloat16
        ).reshape(half_members, block_rows, half_features)
        for step in range((stage_index + 1) * half_lines - 1, stage_index * half_lines - 1, -1):
            side_copy(array, step, cut).start()

    def activate_out(stage_index):
        if stage_index == 0:
            make_share()
        for kind in range(2):
            if stage_index:
                pre_copy(stage_index, kind).wait_recv()
                continue
            for step in range(half_lines):
                level_copy(step, kind).wait_recv()
        weight = half_share(stage_index)

        def one(index, carry):
            columns = tile_at(index)
            up_columns = tile_at(index + hidden_size // TILE)
            gate_pre = own_pre[stage_index, :, columns] + wide(in_pre[stage_index, :, columns])
            up_pre = own_pre[stage_index, :, up_columns] + wide(
                in_pre[stage_index, :, up_columns]
            )
            gate_sigmoid = jax.nn.sigmoid(gate_pre)
            gate_silu = gate_pre * gate_sigmoid
            hidden[:, columns] = (gate_silu * up_pre).astype(jnp.bfloat16)
            own_pre[stage_index, :, columns] = (
                weight * up_pre * gate_sigmoid * (1.0 + gate_pre * (1.0 - gate_sigmoid))
            )
            own_pre[stage_index, :, up_columns] = weight * gate_silu
            return carry

        lax.fori_loop(0, hidden_size // TILE, one, 0)

    def multiply_out(stage_index, cut):
        down_ready()
        value = jnp.dot(
            hidden[...], down[:, cut * half_features:(cut + 1) * half_features],
            preferred_element_type=jnp.float32,
        )
        put_parts(0, cut, stage_index, value * half_share(stage_index))

    def activate_back(stage_index):
        grad_copy(stage_index).wait_recv()

        def one(index, carry):
            columns = tile_at(index)
            up_columns = tile_at(index + hidden_size // TILE)
            grad = own_grad[stage_index, :, columns] + wide(in_grad[stage_index, :, columns])
            pre[:, columns] = (grad * own_pre[stage_index, :, columns]).astype(jnp.bfloat16)
            pre[:, up_columns] = (grad * own_pre[stage_index, :, up_columns]).astype(
                jnp.bfloat16
            )
            return carry

        lax.fori_loop(0, hidden_size // TILE, one, 0)

    def multiply_back(stage_index, cut):
        value = lax.dot_general(
            pre[...], weights[cut * half_features:(cut + 1) * half_features, :],
            (((1,), (1,)), ((), ())), preferred_element_type=jnp.float32,
        )
        put_parts(1, cut, stage_index, value)

    def side_copy(array, step, cut):
        level = level_at(step)
        return remote(
            parts.at[array, cut, level * LANES + other_lane], side.at[array, cut, level],
            side_send.at[array, cut, level], side_recv.at[array, cut, level],
            {"expert": beside},
        )

    def send_sum(array, step, cut, dst, recv, target):
        return remote(
            passing.at[array, cut, step - 1], dst, land_send.at[array, cut, step - 1], recv,
            {"expert": target * LANES + lane},
        )

    def land_copy(array, step, cut, place):
        return send_sum(
            array, step, cut, land.at[array, cut, place], land_recv.at[array, cut, place],
            level_at(step),
        )

    def relay_copy(array, step, cut):
        return send_sum(
            array, step, cut, relayed.at[array, cut, step - half_lines],
            relay_recv.at[array, cut, step - half_lines], level_at(1),
        )

    def pair_sum(array, step, cut):
        side_copy(array, step, cut).wait_recv()
        level = level_at(step)
        return wide(parts[array, cut, level * LANES + lane]) + wide(side[array, cut, level])

    def give_back(array, step, cut):
        def send(copy):
            passing[array, cut, step - 1] = pair_sum(array, step, cut).astype(jnp.bfloat16)
            copy.start()

        if step < half_lines:
            send(land_copy(array, step, cut, 0))
        else:
            pl.when(outer)(lambda: send(relay_copy(array, step, cut)))

    def relay(array, step, cut):
        @pl.when(jnp.logical_not(outer))
        def _():
            value = pair_sum(array, step, cut)
            relay_copy(array, step, cut).wait_recv()
            value = value + wide(relayed[array, cut, step - half_lines])
            passing[array, cut, step - 1] = value.astype(jnp.bfloat16)
            land_copy(array, step, cut, 1).start()

    def cut_columns(cut):
        return pl.ds(cut * half_features, half_features)

    def core_copy(array, cut):
        return remote(
            leaving_core.at[array, cut, pl.ds(other * visitors, visitors)],
            home.at[array, my_group, :, cut_columns(cut)],
            core_send.at[array, cut], core_recv.at[array, cut], {"group": other},
        )

    def core_wait(array, cut):
        remote(
            leaving_core.at[array, cut, pl.ds(my_group * visitors, visitors)],
            home.at[array, other, :, cut_columns(cut)],
            core_send.at[array, cut], core_recv.at[array, cut], {"group": other},
        ).wait_recv()

    def finish(array, cut):
        total = pair_sum(array, 0, cut)
        for place in range(HALVES):
            land_copy(array, 1, cut, place).wait_recv()
            total = total + wide(land[array, cut, place])
        leaving_core[array, cut] = total.astype(jnp.bfloat16)
        core_copy(array, cut).start()
        home[array, my_group, :, cut_columns(cut)] = leaving_core[
            array, cut, pl.ds(my_group * visitors, visitors)
        ]

    def put_home(array, cut):
        core_wait(array, cut)
        found = home[array, :, :, cut_columns(cut)].reshape(block_rows, half_features)
        result[array, :, cut_columns(cut)] = lax.dot_general(
            place_table[...], found, (((0,), (0,)), ((), ())),
            preferred_element_type=jnp.float32,
        ).astype(jnp.bfloat16)

    for array in range(2):
        pair_copy(array).start()

    events = dict(
        gather=gather, separate=separate, multiply_in=multiply_in, multiply_grad=multiply_grad,
        activate_out=activate_out, gather_beside=gather_beside, multiply_level=multiply_level, relay=relay, activate_back=activate_back, multiply_out=multiply_out,
        multiply_back=multiply_back, give_back=give_back, finish=finish,
    )
    for name, *where in SCHEDULE:
        events[name](*where)

    for array in range(2):
        for cut in range(HALVES):
            put_home(array, cut)
    for array in range(2):
        pair_copy(array).wait_send()
        for step in range(lines):
            for index in range(groups):
                forward(sent, array, step, index)
                if BOTH_LANES[array][index]:
                    forward_beside(sent, array, step, index)
        for cut in range(HALVES):
            core_copy(array, cut).wait_send()
            for step in range(lines):
                side_copy(array, step, cut).wait_send()
            for step in range(1, lines):
                land_copy(array, step, cut, 0).wait_send()
    for kind in range(2):
        pre_copy(1, kind).wait_send()
        for step in range(half_lines):
            level_copy(step, kind).wait_send()
    for stage_index in range(HALVES):
        grad_copy(stage_index).wait_send()


def dense_device(tokens, grad_out, expert_ids, gate_score, w_gate_up, w_down):
    groups = lax.axis_size("group")
    members = lax.axis_size("expert")
    per_column, features = tokens.shape
    hidden_size = w_gate_up.shape[3]
    lane_blocks = hidden_size // 128
    gate_rows = jnp.transpose(
        w_gate_up[0].reshape(features, 2, lane_blocks, 128), (0, 2, 1, 3)
    ).reshape(features * lane_blocks * 2, 128)
    down_weights = w_down[0]
    visitors = per_column // groups
    lines = members // LANES
    half_rows = members * per_column // HALVES
    half, full = jnp.bfloat16, jnp.float32
    passes = features // (2 * STRIP)
    chunks = 5 if passes % 5 == 0 else 1
    dma = pltpu.SemaphoreType.DMA
    piece = (groups, visitors, features)
    block = (per_column, features // HALVES)
    vmem = pl.BlockSpec(memory_space=pltpu.VMEM)
    anywhere = pl.BlockSpec(memory_space=pl.ANY)
    found = pl.pallas_call(
        layer_kernel,
        out_shape=jax.ShapeDtypeStruct((2, *tokens.shape), half),
        in_specs=[vmem, vmem, vmem, vmem, anywhere, anywhere],
        out_specs=vmem,
        scratch_shapes=[
            pltpu.VMEM(gate_rows.shape, half),
            pltpu.VMEM((features, 2 * hidden_size), half),
            pltpu.VMEM(down_weights.shape, half),
            pltpu.VMEM((2, *piece), half),
            pltpu.VMEM((2, members, *piece), half),
            pltpu.VMEM((HALVES, half_rows, 2 * hidden_size), full),
            pltpu.VMEM((HALVES, half_rows, hidden_size), full),
            pltpu.VMEM((HALVES, half_rows, 2 * hidden_size), half),
            pltpu.VMEM((HALVES, half_rows, hidden_size), half),
            pltpu.VMEM((HALVES, half_rows, 2 * hidden_size), half),
            pltpu.VMEM((HALVES, half_rows, hidden_size), half),
            pltpu.VMEM((half_rows, hidden_size), half),
            pltpu.VMEM((half_rows, 2 * hidden_size), half),
            pltpu.VMEM((2, HALVES, members, *block), half),
            pltpu.VMEM((2, HALVES, lines, *block), half),
            pltpu.VMEM((2, HALVES, HALVES, *block), half),
            pltpu.VMEM((2, HALVES, lines // HALVES, *block), half),
            pltpu.VMEM((2, HALVES, lines - 1, *block), half),
            pltpu.VMEM((2, HALVES, *block), half),
            pltpu.VMEM((2, *piece), half),
            pltpu.VMEM((members * per_column, 1), full),
            pltpu.VMEM((per_column, per_column), half),
            dma((chunks,)), dma(()), dma((2,)), dma((2,)),
            dma((3, 2, members, groups)), dma((2, members, groups)),
            dma((lines // HALVES, 2)), dma((lines // HALVES, 2)),
            dma((2,)), dma((2,)), dma((HALVES,)), dma((HALVES,)),
            dma((2, HALVES, lines)), dma((2, HALVES, lines)),
            dma((2, HALVES, lines - 1)), dma((2, HALVES, HALVES)),
            dma((2, HALVES, lines // HALVES)),
            dma((2, HALVES)), dma((2, HALVES)),
        ],
        compiler_params=pltpu.CompilerParams(
            collective_id=0, has_side_effects=True, vmem_limit_bytes=58 << 20
        ),
        name="layer",
    )(
        tokens, grad_out, jnp.transpose(expert_ids), jnp.transpose(gate_score),
        gate_rows, down_weights,
    )
    return found[0], found[1]


def on_device(tokens, grad_out, expert_ids, gate_score, w_gate_up, w_down):
    groups = lax.axis_size("group")
    members = lax.axis_size("expert")
    my_group = lax.axis_index("group")
    my_index = lax.axis_index("expert")
    per_column = tokens.shape[0]
    features = tokens.shape[1]
    visitors = per_column // 2
    top_count = expert_ids.shape[1]
    arrivals = groups * visitors
    capacity = min(arrivals, (3 * per_column * top_count + 2 * members - 1) // (2 * members))
    expert_rows = members * capacity
    weights = route_weights(gate_score).reshape(groups, members, per_column, top_count)
    pick_ids = expert_ids.reshape(groups, members, per_column, top_count)
    group_range = jnp.arange(groups, dtype=jnp.int32)
    my_picks = pick_ids[my_group, my_index]
    visits_mine = jnp.any(my_picks[:, :, None] // members == group_range, axis=1)
    leave_table = slot_matrix(visits_mine, visitors).astype(jnp.bfloat16)
    visits_here = jnp.any(pick_ids // members == my_group, axis=3)
    arrival_table = slot_matrix(visits_here[..., None], visitors)[:, :, 0]
    row_ids = jnp.einsum(
        "gest,getk->gesk", arrival_table, pick_ids.astype(jnp.float32), precision=HIGHEST
    )
    row_weights = jnp.einsum("gest,getk->gesk", arrival_table, weights, precision=HIGHEST)
    targets = (my_group * members + jnp.arange(members, dtype=jnp.int32)).astype(jnp.float32)
    matched = row_ids[..., None] == targets
    picked = jnp.any(matched, axis=3)
    picked_weight = jnp.sum(jnp.where(matched, row_weights[..., None], 0.0), axis=3)
    send_flags = picked[:, my_index].reshape(arrivals, members)
    send_table = slot_matrix(send_flags, capacity)
    send_share = jnp.transpose(picked_weight[:, my_index].reshape(arrivals, members))
    send_weight = send_table * send_share[:, None, :]
    came_flags = jnp.transpose(picked[:, :, :, my_index], (1, 0, 2)).reshape(members, arrivals)
    came_table = slot_matrix(came_flags[..., None], capacity)[:, 0]
    came_share = jnp.transpose(picked_weight[:, :, :, my_index], (1, 0, 2)).reshape(
        members, arrivals
    )
    slot_weight = jnp.einsum("ecr,er->ec", came_table, came_share, precision=HIGHEST).reshape(
        expert_rows
    )

    def dispatch(values):
        leaving = jnp.einsum(
            "gst,tf->gsf", leave_table, values, preferred_element_type=jnp.float32
        ).astype(jnp.bfloat16)
        arrived = across(leaving).reshape(arrivals, features)
        onward = jnp.einsum(
            "ecr,rf->ecf",
            send_table.astype(jnp.bfloat16),
            arrived,
            preferred_element_type=jnp.float32,
        ).astype(jnp.bfloat16)
        return within(onward).reshape(expert_rows, features)

    def combine(values, table):
        returned = within(values.reshape(members, capacity, features)).astype(jnp.float32)
        summed = jnp.einsum("ecr,ecf->rf", table, returned, precision=HIGHEST).astype(jnp.bfloat16)
        home = across(summed.reshape(groups, visitors, features))
        return jnp.einsum(
            "gst,gsf->tf", leave_table, home, preferred_element_type=jnp.float32
        ).astype(jnp.bfloat16)

    rows_in = dispatch(tokens)
    rows_grad = dispatch(grad_out)
    gate_weights = w_gate_up[0]
    down_weights = w_down[0]
    partial_value = jnp.einsum(
        "rf,fkh->rkh", rows_in, gate_weights, preferred_element_type=jnp.float32
    )
    grad_partial = jnp.einsum(
        "rf,hf->rh", rows_grad, down_weights, preferred_element_type=jnp.float32
    )
    empty_rows = jnp.zeros((expert_rows, features), jnp.float32)
    gate_both = share_sum(partial_value)
    gate_pre = gate_both[:, 0]
    up_pre = gate_both[:, 1]
    hidden = (jax.nn.silu(gate_pre) * up_pre).astype(jnp.bfloat16)[:, None, :]

    def down_step(running_sum, gathered, first_row):
        return jnp.dot(gathered[:, 0], down_weights, preferred_element_type=jnp.float32)

    expert_out = share_fold(hidden, down_step, empty_rows).astype(jnp.bfloat16)
    hidden_grad = share_sum(grad_partial[:, None, :])[:, 0] * slot_weight[:, None]
    pre_grad = local_grad(gate_pre, up_pre, hidden_grad)

    def input_step(running_sum, gathered, first_row):
        return jnp.einsum("rkh,fkh->rf", gathered, gate_weights, preferred_element_type=jnp.float32)

    expert_grad = share_fold(pre_grad, input_step, empty_rows).astype(jnp.bfloat16)
    layer_out = combine(expert_out, send_weight)
    grad_in = combine(expert_grad, send_table)
    return (layer_out, grad_in)


def per_device(tokens, grad_out, expert_ids, gate_score, w_gate_up, w_down):
    members = lax.axis_size("expert")
    dense = (
        expert_ids.shape[1] == members
        and members == LINES * LANES
        and lax.axis_size("group") == 2
        and lax.axis_size("dp") == 2
        and tokens.shape[0] == 2 * STRIP
        and expert_ids.shape[0] % SPAN == 0
        and tokens.shape[1] % (2 * TILE) == 0
        and w_gate_up.shape[3] % TILE == 0
    )
    plan = dense_device if dense else on_device
    return plan(tokens, grad_out, expert_ids, gate_score, w_gate_up, w_down)


def solution(mesh):
    return jax.shard_map(
        per_device,
        mesh=mesh,
        in_specs=(
            P(("group", "expert"), "dp"),
            P(("group", "expert"), "dp"),
            P(),
            P(),
            P(("group", "expert"), "dp", None, None),
            P(("group", "expert"), None, "dp"),
        ),
        out_specs=(P(("group", "expert"), "dp"), P(("group", "expert"), "dp")),
        check_vma=False,
    )
```

```python
import functools

import jax
import jax.numpy as jnp
from jax import lax
from jax.experimental import pallas as pl
from jax.experimental.pallas import tpu as pltpu
from jax.sharding import PartitionSpec as P

HIGHEST = lax.Precision.HIGHEST


def route_weights(gate_score):
    sigmoid_score = jax.nn.sigmoid(gate_score)
    return 2.5 * sigmoid_score / jnp.sum(sigmoid_score, axis=1, keepdims=True)


def slot_matrix(marked, places):
    count = marked.shape[-2]
    order = jnp.arange(count, dtype=jnp.int32)
    earlier = (order[:, None] >= order[None, :]).astype(jnp.bfloat16)
    running = jnp.einsum(
        "ij,...jk->...ik",
        earlier,
        marked.astype(jnp.bfloat16),
        preferred_element_type=jnp.float32,
    )
    slot_range = jnp.arange(1, places + 1, dtype=jnp.int32).astype(jnp.float32)
    matched = marked[..., None] & (running[..., None] == slot_range)
    return jnp.moveaxis(matched, -3, -1).astype(jnp.float32)


def local_grad(gate_pre, up_pre, hidden_grad):
    sigmoid_gate = jax.nn.sigmoid(gate_pre)
    gate_grad = hidden_grad * up_pre * sigmoid_gate * (1.0 + gate_pre * (1.0 - sigmoid_gate))
    up_grad = hidden_grad * gate_pre * sigmoid_gate
    return jnp.stack([gate_grad, up_grad], axis=1).astype(jnp.bfloat16)


def across(blocks):
    return lax.all_to_all(blocks, "group", split_axis=0, concat_axis=0, tiled=True)


def within(blocks):
    return lax.all_to_all(blocks, "expert", split_axis=0, concat_axis=0, tiled=True)


def share_sum(partial_value):
    return lax.psum_scatter(partial_value, "dp", scatter_dimension=2, tiled=True)


def share_fold(shares, step_fn, start_value):
    return step_fn(start_value, lax.all_gather(shares, "dp", axis=2, tiled=True), jnp.int32(0))


MESH = pl.DeviceIdType.MESH
LANES = 2
TILE = 256
STRIP = 16
HALVES = 2
LINES = 4
SPAN = 128
BOTH_LANES = ((False, False), (False, True))
SCHEDULE = (
    ("gather", 0, 0, 0),
    ("separate", 0),
    ("separate", 1),
    ("gather", 0, 0, 1),
    ("separate", 2),
    ("gather", 1, 0, 1),
    ("separate", 3),
    ("gather", 0, 1, 0),
    ("separate", 4),
    ("multiply_level", 0, 0),
    ("gather", 0, 1, 1),
    ("gather", 0, 2, 1),
    ("multiply_level", 0, 1),
    ("gather", 0, 2, 0),
    ("gather", 1, 1, 1),
    ("gather", 0, 3, 0),
    ("multiply_level", 1, 0),
    ("gather", 0, 3, 1),
    ("gather", 1, 0, 0),
    ("multiply_level", 1, 1),
    ("gather", 1, 2, 0),
    ("gather_beside", 1, 0, 1),
    ("gather", 1, 1, 0),
    ("multiply_in", 1, 0),
    ("gather", 1, 2, 1),
    ("activate_out", 0),
    ("gather", 1, 3, 0),
    ("gather_beside", 1, 1, 1),
    ("multiply_in", 1, 1),
    ("gather", 1, 3, 1),
    ("multiply_out", 0, 0),
    ("multiply_out", 0, 1),
    ("gather_beside", 1, 2, 1),
    ("gather_beside", 1, 3, 1),
    ("multiply_grad", 1),
    ("activate_out", 1),
    ("multiply_out", 1, 0),
    ("give_back", 0, 1, 0),
    ("give_back", 0, 1, 1),
    ("multiply_grad", 0),
    ("multiply_out", 1, 1),
    ("give_back", 0, 3, 0),
    ("activate_back", 1),
    ("give_back", 0, 2, 0),
    ("multiply_back", 1, 0),
    ("give_back", 0, 3, 1),
    ("relay", 0, 3, 0),
    ("multiply_back", 1, 1),
    ("relay", 0, 2, 0),
    ("give_back", 0, 2, 1),
    ("give_back", 1, 3, 0),
    ("activate_back", 0),
    ("relay", 0, 3, 1),
    ("multiply_back", 0, 0),
    ("relay", 0, 2, 1),
    ("give_back", 1, 3, 1),
    ("relay", 1, 3, 0),
    ("give_back", 1, 2, 0),
    ("multiply_back", 0, 1),
    ("give_back", 1, 2, 1),
    ("give_back", 1, 1, 0),
    ("relay", 1, 3, 1),
    ("relay", 1, 2, 0),
    ("give_back", 1, 1, 1),
    ("relay", 1, 2, 1),
    ("finish", 0, 0),
    ("finish", 1, 0),
    ("finish", 0, 1),
    ("put_home", 0, 0),
    ("put_home", 0, 1),
    ("put_home", 1, 0),
    ("finish", 1, 1),
    ("put_home", 1, 1),
)


def visit_order(lines):
    orders = []
    for line in range(lines):
        orders.append(sorted(range(lines), key=lambda level: (abs(level - line), level)))
    for line in range(lines // 2, lines):
        orders[line] = [lines - 1 - level for level in orders[lines - 1 - line]]
    return orders


def layer_kernel(
    tokens_hbm, grad_hbm, ids_hbm, scores_hbm, gate_hbm, down_hbm,
    result,
    tokens, grad_out, ids, scores, stage, weights, down, leaving, rows, own_pre, own_grad, out_pre, out_grad, in_pre, in_grad,
    hidden, pre, parts, side, land, relayed, passing, leaving_core, home, share, place_table,
    input_sem, stage_sem, down_sem, pair_send, pair_recv, row_send, row_recv,
    level_send, level_recv, pre_send, pre_recv, grad_send, grad_recv,
    side_send, side_recv, land_send, land_recv, relay_recv, core_send, core_recv,
):
    my_group = lax.axis_index("group")
    me = lax.axis_index("expert")
    my_share = lax.axis_index("dp")
    other = 1 - my_group
    line, lane = me // LANES, lax.rem(me, LANES)
    other_lane = 1 - lane
    beside = line * LANES + other_lane
    _, groups, visitors, features = leaving.shape
    per_column = tokens.shape[0]
    token_count = ids.shape[1]
    lines = side.shape[2]
    members = lines * LANES
    hidden_size = down.shape[0]
    half_lines = lines // HALVES
    half_members = half_lines * LANES
    block_rows = groups * visitors
    half_rows = half_members * block_rows
    level_rows = LANES * block_rows
    half_features = features // HALVES
    my_half = line // half_lines
    has_up = line < lines - 1
    has_down = line > 0
    outer = jnp.logical_or(line == 0, line == lines - 1)
    orders = visit_order(lines)
    chunks = stage_sem.shape[0]

    def level_at(step):
        return sum(
            (line == place).astype(jnp.int32) * orders[place][step] for place in range(lines)
        )

    def remote(src, dst, send, recv, where):
        return pltpu.make_async_remote_copy(
            src_ref=src, dst_ref=dst, send_sem=send, recv_sem=recv,
            device_id=where, device_id_type=MESH,
        )

    chunk_rows = stage.shape[0] // chunks
    stage_copies = []
    for chunk in range(chunks):
        span = pl.ds(chunk * chunk_rows, chunk_rows)
        stage_copies.append(
            pltpu.make_async_copy(gate_hbm.at[span], stage.at[span], stage_sem.at[chunk])
        )
    down_copy = pltpu.make_async_copy(down_hbm, down, down_sem)

    inputs = ((ids_hbm, ids), (tokens_hbm, tokens), (grad_hbm, grad_out), (scores_hbm, scores))
    input_copies = [
        pltpu.make_async_copy(src, dst, input_sem.at[index])
        for index, (src, dst) in enumerate(inputs)
    ]
    for copy in input_copies:
        copy.start()
    barrier = pltpu.get_barrier_semaphore()

    def hello(where):
        pl.semaphore_signal(barrier, inc=1, device_id=where, device_id_type=MESH)

    hello({"group": other})
    hello({"expert": beside})
    hello({"dp": 1 - my_share})
    for step in range(1, lines - 1):
        hello({"expert": level_at(step) * LANES + lane})
    pl.when(jnp.logical_not(outer))(
        lambda: hello({"expert": level_at(lines - 1) * LANES + lane})
    )
    for copy in stage_copies:
        copy.start()
    down_copy.start()
    for copy in input_copies:
        copy.wait()

    def wide(value):
        return value.astype(jnp.float32)

    def half_dot(left, right):
        return jnp.dot(
            left.astype(jnp.bfloat16), right.astype(jnp.bfloat16),
            preferred_element_type=jnp.float32,
        )

    grouped = wide((ids[0:1, :] >= members).astype(jnp.int32))
    spans = token_count // SPAN
    folded = jnp.concatenate(
        [grouped[:, part * SPAN:(part + 1) * SPAN] for part in range(spans)], axis=0
    )

    def span_iota(shape, dimension):
        return lax.broadcasted_iota(jnp.int32, shape, dimension)

    before, after = span_iota((SPAN, SPAN), 0), span_iota((SPAN, SPAN), 1)
    together = jnp.logical_and(before // per_column == after // per_column, before < after)
    ranked = half_dot(
        jnp.concatenate([1.0 - folded, folded], axis=0), wide(together.astype(jnp.int32))
    )
    rank = jnp.where(folded > 0.5, ranked[spans:], ranked[:spans])
    first_token = (my_group * members + me) * per_column
    span_row = span_iota((spans, SPAN), 0)
    slots = jnp.where(span_row == first_token // SPAN, visitors * folded + rank, 0.0)
    slot = jnp.sum(slots, axis=0, keepdims=True)
    token_of = span_iota((SPAN, per_column), 0)
    column_of = span_iota((SPAN, per_column), 1)
    found_token = token_of == lax.rem(first_token, SPAN) + column_of
    own_slot = half_dot(slot, wide(found_token.astype(jnp.int32)))
    row_of = lax.broadcasted_iota(jnp.int32, (block_rows, per_column), 0)
    place_table[...] = wide((wide(row_of) == own_slot).astype(jnp.int32)).astype(jnp.bfloat16)
    for array, values in enumerate((tokens, grad_out)):
        moved = jnp.dot(
            place_table[...], values[...], preferred_element_type=jnp.float32
        ).astype(jnp.bfloat16)
        for group in range(groups):
            leaving[array, group] = moved[group * visitors:(group + 1) * visitors]
        rows[array, me, my_group] = leaving[array, my_group]

    pl.semaphore_wait(barrier, 3 + lines - 1 - outer.astype(jnp.int32))

    def pair_copy(array):
        return remote(
            leaving.at[array, other], rows.at[array, me, my_group],
            pair_send.at[array], pair_recv.at[array], {"group": other},
        )

    def pair_wait(array):
        remote(
            leaving.at[array, my_group], rows.at[array, me, other],
            pair_send.at[array], pair_recv.at[array], {"group": other},
        ).wait_recv()

    def hop(way, array, block, piece, target):
        where = rows.at[array, block, piece]
        return remote(
            where, where, row_send.at[way, array, block, piece],
            row_recv.at[array, block, piece], {"expert": target},
        )

    def hop_side(array, block, piece):
        return hop(0, array, block, piece, beside)


    def along(act, array, step, block, piece):
        level = level_at(step)
        pl.when(jnp.logical_and(level <= line, has_up))(
            lambda: act(hop(1, array, block, piece, me + LANES))
        )
        pl.when(jnp.logical_and(level >= line, has_down))(
            lambda: act(hop(2, array, block, piece, me - LANES))
        )

    def forward(act, array, step, index):
        piece = piece_at(index)
        block = level_at(step) * LANES + lane
        if step == 0:
            act(hop_side(array, block, piece))
        along(act, array, step, block, piece)
        if step and not BOTH_LANES[array][index]:
            act(hop_side(array, block, piece))

    def forward_beside(act, array, step, index):
        along(act, array, step, level_at(step) * LANES + other_lane, piece_at(index))

    def piece_at(index):
        return my_group if index == 0 else other

    def begin(copy):
        copy.start()

    def sent(copy):
        copy.wait_send()

    def gather(array, step, index):
        piece = piece_at(index)
        mine = level_at(step) * LANES + lane
        if step == 0:
            if index == 1:
                pair_wait(array)
        else:
            hop_side(array, mine, piece).wait_recv()
        forward(begin, array, step, index)

    def gather_beside(array, step, index):
        theirs = level_at(step) * LANES + other_lane
        hop_side(array, theirs, piece_at(index)).wait_recv()
        forward_beside(begin, array, step, index)

    def gathered_level(array, step):
        theirs = level_at(step) * LANES + other_lane
        for index in range(groups):
            if not BOTH_LANES[array][index]:
                hop_side(array, theirs, piece_at(index)).wait_recv()

    def gathered(array, stage_index):
        for step in range(stage_index * half_lines, (stage_index + 1) * half_lines):
            gathered_level(array, step)

    span_rows = STRIP * 2 * (hidden_size // 128)

    def separate(chunk):
        stage_copies[chunk].wait()
        to = lax.broadcasted_iota(jnp.int32, (span_rows, span_rows), 0)
        source = lax.broadcasted_iota(jnp.int32, (span_rows, span_rows), 1)
        per_row = span_rows // STRIP
        select = (source == lax.rem(to, STRIP) * per_row + to // STRIP).astype(jnp.bfloat16)
        passes = chunk_rows // (2 * span_rows)
        unroll = next(count for count in (8, 4, 2, 1) if passes % count == 0)

        def one(index, carry):
            at = chunk * passes + index
            first = pl.multiple_of(at * 2 * span_rows, 2 * span_rows)
            both = jnp.concatenate(
                [stage[pl.ds(first, span_rows)], stage[pl.ds(first + span_rows, span_rows)]],
                axis=1,
            )
            moved = jnp.dot(select, both, preferred_element_type=jnp.float32).astype(jnp.bfloat16)
            base = pl.multiple_of(at * 2 * STRIP, 2 * STRIP)
            for slot_at in range(per_row):
                column = (slot_at % 2) * hidden_size + (slot_at // 2) * 128
                for half in range(2):
                    weights[pl.ds(base + half * STRIP, STRIP), column:column + 128] = moved[
                        slot_at * STRIP:(slot_at + 1) * STRIP, half * 128:(half + 1) * 128
                    ]
            return carry

        lax.fori_loop(0, passes, one, 0, unroll=unroll)

    def half_at(stage_index):
        return my_half if stage_index == 0 else 1 - my_half

    def half_block(array, half):
        found = rows[array, pl.ds(half * half_members, half_members)]
        return found.reshape(half_rows, features)

    def tile_at(index):
        return pl.ds(pl.multiple_of(index * TILE, TILE), TILE)

    def pre_copy(stage_index, kind):
        columns = pl.ds(kind * hidden_size, hidden_size)
        return remote(
            out_pre.at[stage_index, :, columns], in_pre.at[stage_index, :, columns],
            pre_send.at[kind], pre_recv.at[kind],
            {"dp": 1 - my_share},
        )

    def grad_copy(stage_index):
        return remote(
            out_grad.at[stage_index], in_grad.at[stage_index],
            grad_send.at[stage_index], grad_recv.at[stage_index], {"dp": 1 - my_share},
        )

    def level_rows_of(step):
        first = lax.rem(level_at(step), half_lines) * level_rows
        return pl.ds(pl.multiple_of(first, level_rows), level_rows)

    def level_copy(step, kind):
        where = (0, level_rows_of(step), pl.ds(kind * hidden_size, hidden_size))
        return remote(
            out_pre.at[where], in_pre.at[where], level_send.at[step, kind],
            level_recv.at[step, kind], {"dp": 1 - my_share},
        )

    def multiply_level(step, kind):
        if kind == 0:
            gathered_level(0, step)
        columns = pl.ds(kind * hidden_size, hidden_size)
        found = rows[0, pl.ds(level_at(step) * LANES, LANES)].reshape(level_rows, features)
        value = jnp.dot(found, weights[:, columns], preferred_element_type=jnp.float32)
        own_pre[0, level_rows_of(step), columns] = value
        out_pre[0, level_rows_of(step), columns] = value.astype(jnp.bfloat16)
        level_copy(step, kind).start()

    def multiply_in(stage_index, kind):
        if kind == 0:
            gathered(0, stage_index)
        columns = pl.ds(kind * hidden_size, hidden_size)
        value = jnp.dot(
            half_block(0, half_at(stage_index)), weights[:, columns],
            preferred_element_type=jnp.float32,
        )
        own_pre[stage_index, :, columns] = value
        out_pre[stage_index, :, columns] = value.astype(jnp.bfloat16)
        pre_copy(stage_index, kind).start()

    def down_ready():
        if not waited:
            waited.append(True)
            down_copy.wait()

    waited = []

    def multiply_grad(stage_index):
        gathered(1, stage_index)
        down_ready()
        value = lax.dot_general(
            half_block(1, half_at(stage_index)), down[...], (((1,), (1,)), ((), ())),
            preferred_element_type=jnp.float32,
        )
        own_grad[stage_index] = value
        out_grad[stage_index] = value.astype(jnp.bfloat16)
        grad_copy(stage_index).start()

    def make_share():
        score = jax.nn.sigmoid(scores[...])
        weight = 2.5 * score / jnp.sum(score, axis=0, keepdims=True)
        my_expert = my_group * members + me
        mine = jnp.sum(jnp.where(ids[...] == my_expert, weight, 0.0), axis=0, keepdims=True)
        token = lax.broadcasted_iota(jnp.int32, (1, token_count), 1)
        member = lax.rem(token // per_column, members)
        source = token // (per_column * members)
        token_rank = jnp.concatenate([rank[part:part + 1] for part in range(spans)], axis=1)
        row = wide(member * block_rows + source * visitors) + token_rank
        here = grouped == wide(my_group + jnp.zeros((1, token_count), jnp.int32))
        row = jnp.where(here, row, -1.0)
        at = wide(lax.broadcasted_iota(jnp.int32, (HALVES * half_rows, token_count), 0))
        share[...] = jnp.sum(jnp.where(at == row, mine, 0.0), axis=1, keepdims=True)

    def half_share(stage_index):
        first = pl.multiple_of(half_at(stage_index) * half_rows, half_rows)
        return share[pl.ds(first, half_rows), :]

    def put_parts(array, cut, stage_index, value):
        half = half_at(stage_index)
        parts[array, cut, pl.ds(half * half_members, half_members)] = value.astype(
            jnp.bfloat16
        ).reshape(half_members, block_rows, half_features)
        for step in range((stage_index + 1) * half_lines - 1, stage_index * half_lines - 1, -1):
            side_copy(array, step, cut).start()

    def activate_out(stage_index):
        if stage_index == 0:
            make_share()
        for kind in range(2):
            if stage_index:
                pre_copy(stage_index, kind).wait_recv()
                continue
            for step in range(half_lines):
                level_copy(step, kind).wait_recv()
        weight = half_share(stage_index)

        def one(index, carry):
            columns = tile_at(index)
            up_columns = tile_at(index + hidden_size // TILE)
            gate_pre = own_pre[stage_index, :, columns] + wide(in_pre[stage_index, :, columns])
            up_pre = own_pre[stage_index, :, up_columns] + wide(
                in_pre[stage_index, :, up_columns]
            )
            gate_sigmoid = jax.nn.sigmoid(gate_pre)
            gate_silu = gate_pre * gate_sigmoid
            hidden[:, columns] = (gate_silu * up_pre).astype(jnp.bfloat16)
            own_pre[stage_index, :, columns] = (
                weight * up_pre * gate_sigmoid * (1.0 + gate_pre * (1.0 - gate_sigmoid))
            )
            own_pre[stage_index, :, up_columns] = weight * gate_silu
            return carry

        lax.fori_loop(0, hidden_size // TILE, one, 0)

    def multiply_out(stage_index, cut):
        down_ready()
        value = jnp.dot(
            hidden[...], down[:, cut * half_features:(cut + 1) * half_features],
            preferred_element_type=jnp.float32,
        )
        put_parts(0, cut, stage_index, value * half_share(stage_index))

    def activate_back(stage_index):
        grad_copy(stage_index).wait_recv()

        def one(index, carry):
            columns = tile_at(index)
            up_columns = tile_at(index + hidden_size // TILE)
            grad = own_grad[stage_index, :, columns] + wide(in_grad[stage_index, :, columns])
            pre[:, columns] = (grad * own_pre[stage_index, :, columns]).astype(jnp.bfloat16)
            pre[:, up_columns] = (grad * own_pre[stage_index, :, up_columns]).astype(
                jnp.bfloat16
            )
            return carry

        lax.fori_loop(0, hidden_size // TILE, one, 0)

    def multiply_back(stage_index, cut):
        value = lax.dot_general(
            pre[...], weights[cut * half_features:(cut + 1) * half_features, :],
            (((1,), (1,)), ((), ())), preferred_element_type=jnp.float32,
        )
        put_parts(1, cut, stage_index, value)

    def side_copy(array, step, cut):
        level = level_at(step)
        return remote(
            parts.at[array, cut, level * LANES + other_lane], side.at[array, cut, level],
            side_send.at[array, cut, level], side_recv.at[array, cut, level],
            {"expert": beside},
        )

    def send_sum(array, step, cut, dst, recv, target):
        return remote(
            passing.at[array, cut, step - 1], dst, land_send.at[array, cut, step - 1], recv,
            {"expert": target * LANES + lane},
        )

    def land_copy(array, step, cut, place):
        return send_sum(
            array, step, cut, land.at[array, cut, place], land_recv.at[array, cut, place],
            level_at(step),
        )

    def relay_copy(array, step, cut):
        return send_sum(
            array, step, cut, relayed.at[array, cut, step - half_lines],
            relay_recv.at[array, cut, step - half_lines], level_at(1),
        )

    def pair_sum(array, step, cut):
        side_copy(array, step, cut).wait_recv()
        level = level_at(step)
        return wide(parts[array, cut, level * LANES + lane]) + wide(side[array, cut, level])

    def give_back(array, step, cut):
        def send(copy):
            passing[array, cut, step - 1] = pair_sum(array, step, cut).astype(jnp.bfloat16)
            copy.start()

        if step < half_lines:
            send(land_copy(array, step, cut, 0))
        else:
            pl.when(outer)(lambda: send(relay_copy(array, step, cut)))

    def relay(array, step, cut):
        @pl.when(jnp.logical_not(outer))
        def _():
            value = pair_sum(array, step, cut)
            relay_copy(array, step, cut).wait_recv()
            value = value + wide(relayed[array, cut, step - half_lines])
            passing[array, cut, step - 1] = value.astype(jnp.bfloat16)
            land_copy(array, step, cut, 1).start()

    def cut_columns(cut):
        return pl.ds(cut * half_features, half_features)

    def core_copy(array, cut):
        return remote(
            leaving_core.at[array, cut, pl.ds(other * visitors, visitors)],
            home.at[array, my_group, :, cut_columns(cut)],
            core_send.at[array, cut], core_recv.at[array, cut], {"group": other},
        )

    def core_wait(array, cut):
        remote(
            leaving_core.at[array, cut, pl.ds(my_group * visitors, visitors)],
            home.at[array, other, :, cut_columns(cut)],
            core_send.at[array, cut], core_recv.at[array, cut], {"group": other},
        ).wait_recv()

    def finish(array, cut):
        total = pair_sum(array, 0, cut)
        for place in range(HALVES):
            land_copy(array, 1, cut, place).wait_recv()
            total = total + wide(land[array, cut, place])
        leaving_core[array, cut] = total.astype(jnp.bfloat16)
        core_copy(array, cut).start()
        home[array, my_group, :, cut_columns(cut)] = leaving_core[
            array, cut, pl.ds(my_group * visitors, visitors)
        ]

    def put_home(array, cut):
        core_wait(array, cut)
        found = home[array, :, :, cut_columns(cut)].reshape(block_rows, half_features)
        result[array, :, cut_columns(cut)] = lax.dot_general(
            place_table[...], found, (((0,), (0,)), ((), ())),
            preferred_element_type=jnp.float32,
        ).astype(jnp.bfloat16)

    for array in range(2):
        pair_copy(array).start()

    events = dict(
        gather=gather, separate=separate, multiply_in=multiply_in, multiply_grad=multiply_grad,
        activate_out=activate_out, gather_beside=gather_beside, multiply_level=multiply_level, relay=relay, activate_back=activate_back, multiply_out=multiply_out,
        multiply_back=multiply_back, give_back=give_back, finish=finish, put_home=put_home,
    )
    for name, *where in SCHEDULE:
        events[name](*where)

    for array in range(2):
        pair_copy(array).wait_send()
        for step in range(lines):
            for index in range(groups):
                forward(sent, array, step, index)
                if BOTH_LANES[array][index]:
                    forward_beside(sent, array, step, index)
        for cut in range(HALVES):
            core_copy(array, cut).wait_send()
            for step in range(lines):
                side_copy(array, step, cut).wait_send()
            for step in range(1, lines):
                land_copy(array, step, cut, 0).wait_send()
    for kind in range(2):
        pre_copy(1, kind).wait_send()
        for step in range(half_lines):
            level_copy(step, kind).wait_send()
    for stage_index in range(HALVES):
        grad_copy(stage_index).wait_send()


def dense_device(tokens, grad_out, expert_ids, gate_score, w_gate_up, w_down):
    groups = lax.axis_size("group")
    members = lax.axis_size("expert")
    per_column, features = tokens.shape
    hidden_size = w_gate_up.shape[3]
    lane_blocks = hidden_size // 128
    gate_rows = jnp.transpose(
        w_gate_up[0].reshape(features, 2, lane_blocks, 128), (0, 2, 1, 3)
    ).reshape(features * lane_blocks * 2, 128)
    down_weights = w_down[0]
    visitors = per_column // groups
    lines = members // LANES
    half_rows = members * per_column // HALVES
    half, full = jnp.bfloat16, jnp.float32
    passes = features // (2 * STRIP)
    chunks = 5 if passes % 5 == 0 else 1
    dma = pltpu.SemaphoreType.DMA
    piece = (groups, visitors, features)
    block = (per_column, features // HALVES)
    vmem = pl.BlockSpec(memory_space=pltpu.VMEM)
    in_hbm = pl.BlockSpec(memory_space=pltpu.HBM)
    found = pl.pallas_call(
        layer_kernel,
        out_shape=jax.ShapeDtypeStruct((2, *tokens.shape), half),
        in_specs=[in_hbm] * 6,
        out_specs=vmem,
        scratch_shapes=[
            pltpu.VMEM(tokens.shape, half),
            pltpu.VMEM(tokens.shape, half),
            pltpu.VMEM(expert_ids.shape[::-1], jnp.int32),
            pltpu.VMEM(gate_score.shape[::-1], full),
            pltpu.VMEM(gate_rows.shape, half),
            pltpu.VMEM((features, 2 * hidden_size), half),
            pltpu.VMEM(down_weights.shape, half),
            pltpu.VMEM((2, *piece), half),
            pltpu.VMEM((2, members, *piece), half),
            pltpu.VMEM((HALVES, half_rows, 2 * hidden_size), full),
            pltpu.VMEM((HALVES, half_rows, hidden_size), full),
            pltpu.VMEM((HALVES, half_rows, 2 * hidden_size), half),
            pltpu.VMEM((HALVES, half_rows, hidden_size), half),
            pltpu.VMEM((HALVES, half_rows, 2 * hidden_size), half),
            pltpu.VMEM((HALVES, half_rows, hidden_size), half),
            pltpu.VMEM((half_rows, hidden_size), half),
            pltpu.VMEM((half_rows, 2 * hidden_size), half),
            pltpu.VMEM((2, HALVES, members, *block), half),
            pltpu.VMEM((2, HALVES, lines, *block), half),
            pltpu.VMEM((2, HALVES, HALVES, *block), half),
            pltpu.VMEM((2, HALVES, lines // HALVES, *block), half),
            pltpu.VMEM((2, HALVES, lines - 1, *block), half),
            pltpu.VMEM((2, HALVES, *block), half),
            pltpu.VMEM((2, *piece), half),
            pltpu.VMEM((members * per_column, 1), full),
            pltpu.VMEM((per_column, per_column), half),
            dma((4,)), dma((chunks,)), dma(()), dma((2,)), dma((2,)),
            dma((3, 2, members, groups)), dma((2, members, groups)),
            dma((lines // HALVES, 2)), dma((lines // HALVES, 2)),
            dma((2,)), dma((2,)), dma((HALVES,)), dma((HALVES,)),
            dma((2, HALVES, lines)), dma((2, HALVES, lines)),
            dma((2, HALVES, lines - 1)), dma((2, HALVES, HALVES)),
            dma((2, HALVES, lines // HALVES)),
            dma((2, HALVES)), dma((2, HALVES)),
        ],
        compiler_params=pltpu.CompilerParams(
            collective_id=0, has_side_effects=True, vmem_limit_bytes=48 << 20
        ),
        name="layer",
    )(*[
        pltpu.with_memory_space_constraint(value, pltpu.HBM)
        for value in (
            tokens, grad_out, jnp.transpose(expert_ids), jnp.transpose(gate_score),
            gate_rows, down_weights,
        )
    ])
    return found[0], found[1]


def on_device(tokens, grad_out, expert_ids, gate_score, w_gate_up, w_down):
    groups = lax.axis_size("group")
    members = lax.axis_size("expert")
    my_group = lax.axis_index("group")
    my_index = lax.axis_index("expert")
    per_column = tokens.shape[0]
    features = tokens.shape[1]
    visitors = per_column // 2
    top_count = expert_ids.shape[1]
    arrivals = groups * visitors
    capacity = min(arrivals, (3 * per_column * top_count + 2 * members - 1) // (2 * members))
    expert_rows = members * capacity
    weights = route_weights(gate_score).reshape(groups, members, per_column, top_count)
    pick_ids = expert_ids.reshape(groups, members, per_column, top_count)
    group_range = jnp.arange(groups, dtype=jnp.int32)
    my_picks = pick_ids[my_group, my_index]
    visits_mine = jnp.any(my_picks[:, :, None] // members == group_range, axis=1)
    leave_table = slot_matrix(visits_mine, visitors).astype(jnp.bfloat16)
    visits_here = jnp.any(pick_ids // members == my_group, axis=3)
    arrival_table = slot_matrix(visits_here[..., None], visitors)[:, :, 0]
    row_ids = jnp.einsum(
        "gest,getk->gesk", arrival_table, pick_ids.astype(jnp.float32), precision=HIGHEST
    )
    row_weights = jnp.einsum("gest,getk->gesk", arrival_table, weights, precision=HIGHEST)
    targets = (my_group * members + jnp.arange(members, dtype=jnp.int32)).astype(jnp.float32)
    matched = row_ids[..., None] == targets
    picked = jnp.any(matched, axis=3)
    picked_weight = jnp.sum(jnp.where(matched, row_weights[..., None], 0.0), axis=3)
    send_flags = picked[:, my_index].reshape(arrivals, members)
    send_table = slot_matrix(send_flags, capacity)
    send_share = jnp.transpose(picked_weight[:, my_index].reshape(arrivals, members))
    send_weight = send_table * send_share[:, None, :]
    came_flags = jnp.transpose(picked[:, :, :, my_index], (1, 0, 2)).reshape(members, arrivals)
    came_table = slot_matrix(came_flags[..., None], capacity)[:, 0]
    came_share = jnp.transpose(picked_weight[:, :, :, my_index], (1, 0, 2)).reshape(
        members, arrivals
    )
    slot_weight = jnp.einsum("ecr,er->ec", came_table, came_share, precision=HIGHEST).reshape(
        expert_rows
    )

    def dispatch(values):
        leaving = jnp.einsum(
            "gst,tf->gsf", leave_table, values, preferred_element_type=jnp.float32
        ).astype(jnp.bfloat16)
        arrived = across(leaving).reshape(arrivals, features)
        onward = jnp.einsum(
            "ecr,rf->ecf",
            send_table.astype(jnp.bfloat16),
            arrived,
            preferred_element_type=jnp.float32,
        ).astype(jnp.bfloat16)
        return within(onward).reshape(expert_rows, features)

    def combine(values, table):
        returned = within(values.reshape(members, capacity, features)).astype(jnp.float32)
        summed = jnp.einsum("ecr,ecf->rf", table, returned, precision=HIGHEST).astype(jnp.bfloat16)
        home = across(summed.reshape(groups, visitors, features))
        return jnp.einsum(
            "gst,gsf->tf", leave_table, home, preferred_element_type=jnp.float32
        ).astype(jnp.bfloat16)

    rows_in = dispatch(tokens)
    rows_grad = dispatch(grad_out)
    gate_weights = w_gate_up[0]
    down_weights = w_down[0]
    partial_value = jnp.einsum(
        "rf,fkh->rkh", rows_in, gate_weights, preferred_element_type=jnp.float32
    )
    grad_partial = jnp.einsum(
        "rf,hf->rh", rows_grad, down_weights, preferred_element_type=jnp.float32
    )
    empty_rows = jnp.zeros((expert_rows, features), jnp.float32)
    gate_both = share_sum(partial_value)
    gate_pre = gate_both[:, 0]
    up_pre = gate_both[:, 1]
    hidden = (jax.nn.silu(gate_pre) * up_pre).astype(jnp.bfloat16)[:, None, :]

    def down_step(running_sum, gathered, first_row):
        return jnp.dot(gathered[:, 0], down_weights, preferred_element_type=jnp.float32)

    expert_out = share_fold(hidden, down_step, empty_rows).astype(jnp.bfloat16)
    hidden_grad = share_sum(grad_partial[:, None, :])[:, 0] * slot_weight[:, None]
    pre_grad = local_grad(gate_pre, up_pre, hidden_grad)

    def input_step(running_sum, gathered, first_row):
        return jnp.einsum("rkh,fkh->rf", gathered, gate_weights, preferred_element_type=jnp.float32)

    expert_grad = share_fold(pre_grad, input_step, empty_rows).astype(jnp.bfloat16)
    layer_out = combine(expert_out, send_weight)
    grad_in = combine(expert_grad, send_table)
    return (layer_out, grad_in)


def per_device(tokens, grad_out, expert_ids, gate_score, w_gate_up, w_down):
    members = lax.axis_size("expert")
    dense = (
        expert_ids.shape[1] == members
        and members == LINES * LANES
        and lax.axis_size("group") == 2
        and lax.axis_size("dp") == 2
        and tokens.shape[0] == 2 * STRIP
        and expert_ids.shape[0] % SPAN == 0
        and tokens.shape[1] % (2 * TILE) == 0
        and w_gate_up.shape[3] % TILE == 0
    )
    plan = dense_device if dense else on_device
    return plan(tokens, grad_out, expert_ids, gate_score, w_gate_up, w_down)


def solution(mesh):
    return jax.shard_map(
        per_device,
        mesh=mesh,
        in_specs=(
            P(("group", "expert"), "dp"),
            P(("group", "expert"), "dp"),
            P(),
            P(),
            P(("group", "expert"), "dp", None, None),
            P(("group", "expert"), None, "dp"),
        ),
        out_specs=(P(("group", "expert"), "dp"), P(("group", "expert"), "dp")),
        check_vma=False,
    )
```

```python
import functools

import jax
import jax.numpy as jnp
from jax import lax
from jax.experimental import pallas as pl
from jax.experimental.pallas import tpu as pltpu
from jax.sharding import PartitionSpec as P

HIGHEST = lax.Precision.HIGHEST


def route_weights(gate_score):
    sigmoid_score = jax.nn.sigmoid(gate_score)
    return 2.5 * sigmoid_score / jnp.sum(sigmoid_score, axis=1, keepdims=True)


def slot_matrix(marked, places):
    count = marked.shape[-2]
    order = jnp.arange(count, dtype=jnp.int32)
    earlier = (order[:, None] >= order[None, :]).astype(jnp.bfloat16)
    running = jnp.einsum(
        "ij,...jk->...ik",
        earlier,
        marked.astype(jnp.bfloat16),
        preferred_element_type=jnp.float32,
    )
    slot_range = jnp.arange(1, places + 1, dtype=jnp.int32).astype(jnp.float32)
    matched = marked[..., None] & (running[..., None] == slot_range)
    return jnp.moveaxis(matched, -3, -1).astype(jnp.float32)


def local_grad(gate_pre, up_pre, hidden_grad):
    sigmoid_gate = jax.nn.sigmoid(gate_pre)
    gate_grad = hidden_grad * up_pre * sigmoid_gate * (1.0 + gate_pre * (1.0 - sigmoid_gate))
    up_grad = hidden_grad * gate_pre * sigmoid_gate
    return jnp.stack([gate_grad, up_grad], axis=1).astype(jnp.bfloat16)


def across(blocks):
    return lax.all_to_all(blocks, "group", split_axis=0, concat_axis=0, tiled=True)


def within(blocks):
    return lax.all_to_all(blocks, "expert", split_axis=0, concat_axis=0, tiled=True)


def share_sum(partial_value):
    return lax.psum_scatter(partial_value, "dp", scatter_dimension=2, tiled=True)


def share_fold(shares, step_fn, start_value):
    return step_fn(start_value, lax.all_gather(shares, "dp", axis=2, tiled=True), jnp.int32(0))


MESH = pl.DeviceIdType.MESH
LANES = 2
TILE = 256
STRIP = 16
HALVES = 2
LINES = 4
SPAN = 128
BOTH_LANES = ((False, False), (True, False))
SCHEDULE = (
    ("gather", 0, 0, 0),
    ("separate", 0),
    ("gather", 0, 0, 1),
    ("gather", 1, 0, 0),
    ("separate", 1),
    ("separate", 2),
    ("gather", 0, 1, 0),
    ("separate", 3),
    ("separate", 4),
    ("gather", 0, 1, 1),
    ("multiply_level", 0, 0),
    ("gather", 0, 2, 0),
    ("multiply_level", 0, 1),
    ("gather", 0, 2, 1),
    ("gather", 0, 3, 0),
    ("multiply_level", 1, 0),
    ("gather", 0, 3, 1),
    ("gather", 1, 0, 1),
    ("multiply_level", 1, 1),
    ("gather", 1, 2, 0),
    ("gather_beside", 1, 0, 0),
    ("multiply_in", 1, 0),
    ("gather", 1, 1, 1),
    ("multiply_in", 1, 1),
    ("gather", 1, 1, 0),
    ("gather", 1, 2, 1),
    ("activate_out", 0),
    ("gather", 1, 3, 1),
    ("gather_beside", 1, 1, 0),
    ("multiply_out", 0, 0),
    ("gather", 1, 3, 0),
    ("multiply_out", 0, 1),
    ("gather_beside", 1, 2, 0),
    ("gather_beside", 1, 3, 0),
    ("multiply_grad", 1),
    ("activate_out", 1),
    ("multiply_out", 1, 0),
    ("give_back", 0, 1, 0),
    ("give_back", 0, 1, 1),
    ("multiply_grad", 0),
    ("multiply_out", 1, 1),
    ("give_back", 0, 3, 0),
    ("activate_back", 1),
    ("give_back", 0, 2, 0),
    ("multiply_back", 1, 0),
    ("give_back", 0, 3, 1),
    ("give_back", 0, 2, 1),
    ("multiply_back", 1, 1),
    ("relay", 0, 3, 0),
    ("activate_back", 0),
    ("give_back", 1, 3, 0),
    ("relay", 0, 2, 0),
    ("give_back", 1, 2, 0),
    ("multiply_back", 0, 0),
    ("relay", 0, 3, 1),
    ("relay", 0, 2, 1),
    ("give_back", 1, 3, 1),
    ("multiply_back", 0, 1),
    ("relay", 1, 3, 0),
    ("give_back", 1, 2, 1),
    ("give_back", 1, 1, 0),
    ("relay", 1, 2, 0),
    ("relay", 1, 3, 1),
    ("finish", 0, 0),
    ("finish", 0, 1),
    ("give_back", 1, 1, 1),
    ("relay", 1, 2, 1),
    ("finish", 1, 0),
    ("put_home", 0, 0),
    ("put_home", 0, 1),
    ("put_home", 1, 0),
    ("finish", 1, 1),
    ("put_home", 1, 1),
)


def visit_order(lines):
    orders = []
    for line in range(lines):
        orders.append(sorted(range(lines), key=lambda level: (abs(level - line), level)))
    for line in range(lines // 2, lines):
        orders[line] = [lines - 1 - level for level in orders[lines - 1 - line]]
    return orders


def layer_kernel(
    tokens_hbm, grad_hbm, ids_hbm, scores_hbm, gate_hbm, down_hbm,
    result,
    tokens, grad_out, ids, scores, stage, weights, down, leaving, rows, own_pre, own_grad, out_pre, out_grad, in_pre, in_grad,
    hidden, pre, parts, side, land, relayed, passing, leaving_core, home, share, place_table,
    input_sem, stage_sem, down_sem, pair_send, pair_recv, row_send, row_recv,
    level_send, level_recv, pre_send, pre_recv, grad_send, grad_recv,
    side_send, side_recv, land_send, land_recv, relay_recv, core_send, core_recv,
):
    my_group = lax.axis_index("group")
    me = lax.axis_index("expert")
    my_share = lax.axis_index("dp")
    other = 1 - my_group
    line, lane = me // LANES, lax.rem(me, LANES)
    other_lane = 1 - lane
    beside = line * LANES + other_lane
    _, groups, visitors, features = leaving.shape
    per_column = tokens.shape[0]
    token_count = ids.shape[1]
    lines = side.shape[2]
    members = lines * LANES
    hidden_size = down.shape[0]
    half_lines = lines // HALVES
    half_members = half_lines * LANES
    block_rows = groups * visitors
    half_rows = half_members * block_rows
    level_rows = LANES * block_rows
    half_features = features // HALVES
    my_half = line // half_lines
    has_up = line < lines - 1
    has_down = line > 0
    outer = jnp.logical_or(line == 0, line == lines - 1)
    orders = visit_order(lines)
    chunks = stage_sem.shape[0]

    def level_at(step):
        return sum(
            (line == place).astype(jnp.int32) * orders[place][step] for place in range(lines)
        )

    def remote(src, dst, send, recv, where):
        return pltpu.make_async_remote_copy(
            src_ref=src, dst_ref=dst, send_sem=send, recv_sem=recv,
            device_id=where, device_id_type=MESH,
        )

    chunk_rows = stage.shape[0] // chunks
    stage_copies = []
    for chunk in range(chunks):
        span = pl.ds(chunk * chunk_rows, chunk_rows)
        stage_copies.append(
            pltpu.make_async_copy(gate_hbm.at[span], stage.at[span], stage_sem.at[chunk])
        )
    down_copy = pltpu.make_async_copy(down_hbm, down, down_sem)

    inputs = ((ids_hbm, ids), (tokens_hbm, tokens), (grad_hbm, grad_out), (scores_hbm, scores))
    input_copies = [
        pltpu.make_async_copy(src, dst, input_sem.at[index])
        for index, (src, dst) in enumerate(inputs)
    ]
    for copy in input_copies:
        copy.start()
    barrier = pltpu.get_barrier_semaphore()

    def hello(where):
        pl.semaphore_signal(barrier, inc=1, device_id=where, device_id_type=MESH)

    hello({"group": other})
    hello({"expert": beside})
    hello({"dp": 1 - my_share})
    for step in range(1, lines - 1):
        hello({"expert": level_at(step) * LANES + lane})
    pl.when(jnp.logical_not(outer))(
        lambda: hello({"expert": level_at(lines - 1) * LANES + lane})
    )
    for copy in stage_copies:
        copy.start()
    down_copy.start()
    for copy in input_copies:
        copy.wait()

    def wide(value):
        return value.astype(jnp.float32)

    def half_dot(left, right):
        return jnp.dot(
            left.astype(jnp.bfloat16), right.astype(jnp.bfloat16),
            preferred_element_type=jnp.float32,
        )

    grouped = wide((ids[0:1, :] >= members).astype(jnp.int32))
    spans = token_count // SPAN
    folded = jnp.concatenate(
        [grouped[:, part * SPAN:(part + 1) * SPAN] for part in range(spans)], axis=0
    )

    def span_iota(shape, dimension):
        return lax.broadcasted_iota(jnp.int32, shape, dimension)

    before, after = span_iota((SPAN, SPAN), 0), span_iota((SPAN, SPAN), 1)
    together = jnp.logical_and(before // per_column == after // per_column, before < after)
    ranked = half_dot(
        jnp.concatenate([1.0 - folded, folded], axis=0), wide(together.astype(jnp.int32))
    )
    rank = jnp.where(folded > 0.5, ranked[spans:], ranked[:spans])
    first_token = (my_group * members + me) * per_column
    span_row = span_iota((spans, SPAN), 0)
    slots = jnp.where(span_row == first_token // SPAN, visitors * folded + rank, 0.0)
    slot = jnp.sum(slots, axis=0, keepdims=True)
    token_of = span_iota((SPAN, per_column), 0)
    column_of = span_iota((SPAN, per_column), 1)
    found_token = token_of == lax.rem(first_token, SPAN) + column_of
    own_slot = half_dot(slot, wide(found_token.astype(jnp.int32)))
    row_of = lax.broadcasted_iota(jnp.int32, (block_rows, per_column), 0)
    place_table[...] = wide((wide(row_of) == own_slot).astype(jnp.int32)).astype(jnp.bfloat16)
    for array, values in enumerate((tokens, grad_out)):
        moved = jnp.dot(
            place_table[...], values[...], preferred_element_type=jnp.float32
        ).astype(jnp.bfloat16)
        for group in range(groups):
            leaving[array, group] = moved[group * visitors:(group + 1) * visitors]
        rows[array, me, my_group] = leaving[array, my_group]

    pl.semaphore_wait(barrier, 3 + lines - 1 - outer.astype(jnp.int32))

    def pair_copy(array):
        return remote(
            leaving.at[array, other], rows.at[array, me, my_group],
            pair_send.at[array], pair_recv.at[array], {"group": other},
        )

    def pair_wait(array):
        remote(
            leaving.at[array, my_group], rows.at[array, me, other],
            pair_send.at[array], pair_recv.at[array], {"group": other},
        ).wait_recv()

    def hop(way, array, block, piece, target):
        where = rows.at[array, block, piece]
        return remote(
            where, where, row_send.at[way, array, block, piece],
            row_recv.at[array, block, piece], {"expert": target},
        )

    def hop_side(array, block, piece):
        return hop(0, array, block, piece, beside)


    def along(act, array, step, block, piece):
        level = level_at(step)
        pl.when(jnp.logical_and(level <= line, has_up))(
            lambda: act(hop(1, array, block, piece, me + LANES))
        )
        pl.when(jnp.logical_and(level >= line, has_down))(
            lambda: act(hop(2, array, block, piece, me - LANES))
        )

    def forward(act, array, step, index):
        piece = piece_at(index)
        block = level_at(step) * LANES + lane
        if step == 0:
            act(hop_side(array, block, piece))
        along(act, array, step, block, piece)
        if step and not BOTH_LANES[array][index]:
            act(hop_side(array, block, piece))

    def forward_beside(act, array, step, index):
        along(act, array, step, level_at(step) * LANES + other_lane, piece_at(index))

    def piece_at(index):
        return my_group if index == 0 else other

    def begin(copy):
        copy.start()

    def sent(copy):
        copy.wait_send()

    def gather(array, step, index):
        piece = piece_at(index)
        mine = level_at(step) * LANES + lane
        if step == 0:
            if index == 1:
                pair_wait(array)
        else:
            hop_side(array, mine, piece).wait_recv()
        forward(begin, array, step, index)

    def gather_beside(array, step, index):
        theirs = level_at(step) * LANES + other_lane
        hop_side(array, theirs, piece_at(index)).wait_recv()
        forward_beside(begin, array, step, index)

    def gathered_level(array, step):
        theirs = level_at(step) * LANES + other_lane
        for index in range(groups):
            if not BOTH_LANES[array][index]:
                hop_side(array, theirs, piece_at(index)).wait_recv()

    def gathered(array, stage_index):
        for step in range(stage_index * half_lines, (stage_index + 1) * half_lines):
            gathered_level(array, step)

    span_rows = STRIP * 2 * (hidden_size // 128)

    def separate(chunk):
        stage_copies[chunk].wait()
        to = lax.broadcasted_iota(jnp.int32, (span_rows, span_rows), 0)
        source = lax.broadcasted_iota(jnp.int32, (span_rows, span_rows), 1)
        per_row = span_rows // STRIP
        select = (source == lax.rem(to, STRIP) * per_row + to // STRIP).astype(jnp.bfloat16)
        passes = chunk_rows // (2 * span_rows)
        unroll = next(count for count in (8, 4, 2, 1) if passes % count == 0)

        def one(index, carry):
            at = chunk * passes + index
            first = pl.multiple_of(at * 2 * span_rows, 2 * span_rows)
            both = jnp.concatenate(
                [stage[pl.ds(first, span_rows)], stage[pl.ds(first + span_rows, span_rows)]],
                axis=1,
            )
            moved = jnp.dot(select, both, preferred_element_type=jnp.float32).astype(jnp.bfloat16)
            base = pl.multiple_of(at * 2 * STRIP, 2 * STRIP)
            for slot_at in range(per_row):
                column = (slot_at % 2) * hidden_size + (slot_at // 2) * 128
                for half in range(2):
                    weights[pl.ds(base + half * STRIP, STRIP), column:column + 128] = moved[
                        slot_at * STRIP:(slot_at + 1) * STRIP, half * 128:(half + 1) * 128
                    ]
            return carry

        lax.fori_loop(0, passes, one, 0, unroll=unroll)

    def half_at(stage_index):
        return my_half if stage_index == 0 else 1 - my_half

    def half_block(array, half):
        found = rows[array, pl.ds(half * half_members, half_members)]
        return found.reshape(half_rows, features)

    def tile_at(index):
        return pl.ds(pl.multiple_of(index * TILE, TILE), TILE)

    def pre_copy(stage_index, kind):
        columns = pl.ds(kind * hidden_size, hidden_size)
        return remote(
            out_pre.at[stage_index, :, columns], in_pre.at[stage_index, :, columns],
            pre_send.at[kind], pre_recv.at[kind],
            {"dp": 1 - my_share},
        )

    def grad_copy(stage_index):
        return remote(
            out_grad.at[stage_index], in_grad.at[stage_index],
            grad_send.at[stage_index], grad_recv.at[stage_index], {"dp": 1 - my_share},
        )

    def level_rows_of(step):
        first = lax.rem(level_at(step), half_lines) * level_rows
        return pl.ds(pl.multiple_of(first, level_rows), level_rows)

    def level_copy(step, kind):
        where = (0, level_rows_of(step), pl.ds(kind * hidden_size, hidden_size))
        return remote(
            out_pre.at[where], in_pre.at[where], level_send.at[step, kind],
            level_recv.at[step, kind], {"dp": 1 - my_share},
        )

    def multiply_level(step, kind):
        if kind == 0:
            gathered_level(0, step)
        columns = pl.ds(kind * hidden_size, hidden_size)
        found = rows[0, pl.ds(level_at(step) * LANES, LANES)].reshape(level_rows, features)
        value = jnp.dot(found, weights[:, columns], preferred_element_type=jnp.float32)
        own_pre[0, level_rows_of(step), columns] = value
        out_pre[0, level_rows_of(step), columns] = value.astype(jnp.bfloat16)
        level_copy(step, kind).start()

    def multiply_in(stage_index, kind):
        if kind == 0:
            gathered(0, stage_index)
        columns = pl.ds(kind * hidden_size, hidden_size)
        value = jnp.dot(
            half_block(0, half_at(stage_index)), weights[:, columns],
            preferred_element_type=jnp.float32,
        )
        own_pre[stage_index, :, columns] = value
        out_pre[stage_index, :, columns] = value.astype(jnp.bfloat16)
        pre_copy(stage_index, kind).start()

    def down_ready():
        if not waited:
            waited.append(True)
            down_copy.wait()

    waited = []

    def multiply_grad(stage_index):
        gathered(1, stage_index)
        down_ready()
        value = lax.dot_general(
            half_block(1, half_at(stage_index)), down[...], (((1,), (1,)), ((), ())),
            preferred_element_type=jnp.float32,
        )
        own_grad[stage_index] = value
        out_grad[stage_index] = value.astype(jnp.bfloat16)
        grad_copy(stage_index).start()

    def make_share():
        score = jax.nn.sigmoid(scores[...])
        weight = 2.5 * score / jnp.sum(score, axis=0, keepdims=True)
        my_expert = my_group * members + me
        mine = jnp.sum(jnp.where(ids[...] == my_expert, weight, 0.0), axis=0, keepdims=True)
        token = lax.broadcasted_iota(jnp.int32, (1, token_count), 1)
        member = lax.rem(token // per_column, members)
        source = token // (per_column * members)
        token_rank = jnp.concatenate([rank[part:part + 1] for part in range(spans)], axis=1)
        row = wide(member * block_rows + source * visitors) + token_rank
        here = grouped == wide(my_group + jnp.zeros((1, token_count), jnp.int32))
        row = jnp.where(here, row, -1.0)
        at = wide(lax.broadcasted_iota(jnp.int32, (HALVES * half_rows, token_count), 0))
        share[...] = jnp.sum(jnp.where(at == row, mine, 0.0), axis=1, keepdims=True)

    def half_share(stage_index):
        first = pl.multiple_of(half_at(stage_index) * half_rows, half_rows)
        return share[pl.ds(first, half_rows), :]

    def put_parts(array, cut, stage_index, value):
        half = half_at(stage_index)
        parts[array, cut, pl.ds(half * half_members, half_members)] = value.astype(
            jnp.bfloat16
        ).reshape(half_members, block_rows, half_features)
        for step in range((stage_index + 1) * half_lines - 1, stage_index * half_lines - 1, -1):
            side_copy(array, step, cut).start()

    def activate_out(stage_index):
        if stage_index == 0:
            make_share()
        for kind in range(2):
            if stage_index:
                pre_copy(stage_index, kind).wait_recv()
                continue
            for step in range(half_lines):
                level_copy(step, kind).wait_recv()
        weight = half_share(stage_index)

        def one(index, carry):
            columns = tile_at(index)
            up_columns = tile_at(index + hidden_size // TILE)
            gate_pre = own_pre[stage_index, :, columns] + wide(in_pre[stage_index, :, columns])
            up_pre = own_pre[stage_index, :, up_columns] + wide(
                in_pre[stage_index, :, up_columns]
            )
            gate_sigmoid = jax.nn.sigmoid(gate_pre)
            gate_silu = gate_pre * gate_sigmoid
            hidden[:, columns] = (gate_silu * up_pre).astype(jnp.bfloat16)
            own_pre[stage_index, :, columns] = (
                weight * up_pre * gate_sigmoid * (1.0 + gate_pre * (1.0 - gate_sigmoid))
            )
            own_pre[stage_index, :, up_columns] = weight * gate_silu
            return carry

        lax.fori_loop(0, hidden_size // TILE, one, 0)

    def multiply_out(stage_index, cut):
        down_ready()
        value = jnp.dot(
            hidden[...], down[:, cut * half_features:(cut + 1) * half_features],
            preferred_element_type=jnp.float32,
        )
        put_parts(0, cut, stage_index, value * half_share(stage_index))

    def activate_back(stage_index):
        grad_copy(stage_index).wait_recv()

        def one(index, carry):
            columns = tile_at(index)
            up_columns = tile_at(index + hidden_size // TILE)
            grad = own_grad[stage_index, :, columns] + wide(in_grad[stage_index, :, columns])
            pre[:, columns] = (grad * own_pre[stage_index, :, columns]).astype(jnp.bfloat16)
            pre[:, up_columns] = (grad * own_pre[stage_index, :, up_columns]).astype(
                jnp.bfloat16
            )
            return carry

        lax.fori_loop(0, hidden_size // TILE, one, 0)

    def multiply_back(stage_index, cut):
        value = lax.dot_general(
            pre[...], weights[cut * half_features:(cut + 1) * half_features, :],
            (((1,), (1,)), ((), ())), preferred_element_type=jnp.float32,
        )
        put_parts(1, cut, stage_index, value)

    def side_copy(array, step, cut):
        level = level_at(step)
        return remote(
            parts.at[array, cut, level * LANES + other_lane], side.at[array, cut, level],
            side_send.at[array, cut, level], side_recv.at[array, cut, level],
            {"expert": beside},
        )

    def send_sum(array, step, cut, dst, recv, target):
        return remote(
            passing.at[array, cut, step - 1], dst, land_send.at[array, cut, step - 1], recv,
            {"expert": target * LANES + lane},
        )

    def land_copy(array, step, cut, place):
        return send_sum(
            array, step, cut, land.at[array, cut, place], land_recv.at[array, cut, place],
            level_at(step),
        )

    def relay_copy(array, step, cut):
        return send_sum(
            array, step, cut, relayed.at[array, cut, step - half_lines],
            relay_recv.at[array, cut, step - half_lines], level_at(1),
        )

    def pair_sum(array, step, cut):
        side_copy(array, step, cut).wait_recv()
        level = level_at(step)
        return wide(parts[array, cut, level * LANES + lane]) + wide(side[array, cut, level])

    def give_back(array, step, cut):
        def send(copy):
            passing[array, cut, step - 1] = pair_sum(array, step, cut).astype(jnp.bfloat16)
            copy.start()

        if step < half_lines:
            send(land_copy(array, step, cut, 0))
        else:
            pl.when(outer)(lambda: send(relay_copy(array, step, cut)))

    def relay(array, step, cut):
        @pl.when(jnp.logical_not(outer))
        def _():
            value = pair_sum(array, step, cut)
            relay_copy(array, step, cut).wait_recv()
            value = value + wide(relayed[array, cut, step - half_lines])
            passing[array, cut, step - 1] = value.astype(jnp.bfloat16)
            land_copy(array, step, cut, 1).start()

    def cut_columns(cut):
        return pl.ds(cut * half_features, half_features)

    def core_copy(array, cut):
        return remote(
            leaving_core.at[array, cut, pl.ds(other * visitors, visitors)],
            home.at[array, my_group, :, cut_columns(cut)],
            core_send.at[array, cut], core_recv.at[array, cut], {"group": other},
        )

    def core_wait(array, cut):
        remote(
            leaving_core.at[array, cut, pl.ds(my_group * visitors, visitors)],
            home.at[array, other, :, cut_columns(cut)],
            core_send.at[array, cut], core_recv.at[array, cut], {"group": other},
        ).wait_recv()

    def finish(array, cut):
        total = pair_sum(array, 0, cut)
        for place in range(HALVES):
            land_copy(array, 1, cut, place).wait_recv()
            total = total + wide(land[array, cut, place])
        leaving_core[array, cut] = total.astype(jnp.bfloat16)
        core_copy(array, cut).start()
        home[array, my_group, :, cut_columns(cut)] = leaving_core[
            array, cut, pl.ds(my_group * visitors, visitors)
        ]

    def put_home(array, cut):
        core_wait(array, cut)
        found = home[array, :, :, cut_columns(cut)].reshape(block_rows, half_features)
        result[array, :, cut_columns(cut)] = lax.dot_general(
            place_table[...], found, (((0,), (0,)), ((), ())),
            preferred_element_type=jnp.float32,
        ).astype(jnp.bfloat16)

    for array in range(2):
        pair_copy(array).start()

    events = dict(
        gather=gather, separate=separate, multiply_in=multiply_in, multiply_grad=multiply_grad,
        activate_out=activate_out, gather_beside=gather_beside, multiply_level=multiply_level, relay=relay, activate_back=activate_back, multiply_out=multiply_out,
        multiply_back=multiply_back, give_back=give_back, finish=finish, put_home=put_home,
    )
    for name, *where in SCHEDULE:
        events[name](*where)

    for array in range(2):
        pair_copy(array).wait_send()
        for step in range(lines):
            for index in range(groups):
                forward(sent, array, step, index)
                if BOTH_LANES[array][index]:
                    forward_beside(sent, array, step, index)
        for cut in range(HALVES):
            core_copy(array, cut).wait_send()
            for step in range(lines):
                side_copy(array, step, cut).wait_send()
            for step in range(1, lines):
                land_copy(array, step, cut, 0).wait_send()
    for kind in range(2):
        pre_copy(1, kind).wait_send()
        for step in range(half_lines):
            level_copy(step, kind).wait_send()
    for stage_index in range(HALVES):
        grad_copy(stage_index).wait_send()


def dense_device(tokens, grad_out, expert_ids, gate_score, w_gate_up, w_down):
    groups = lax.axis_size("group")
    members = lax.axis_size("expert")
    per_column, features = tokens.shape
    hidden_size = w_gate_up.shape[3]
    lane_blocks = hidden_size // 128
    gate_rows = jnp.transpose(
        w_gate_up[0].reshape(features, 2, lane_blocks, 128), (0, 2, 1, 3)
    ).reshape(features * lane_blocks * 2, 128)
    down_weights = w_down[0]
    visitors = per_column // groups
    lines = members // LANES
    half_rows = members * per_column // HALVES
    half, full = jnp.bfloat16, jnp.float32
    passes = features // (2 * STRIP)
    chunks = 5 if passes % 5 == 0 else 1
    dma = pltpu.SemaphoreType.DMA
    piece = (groups, visitors, features)
    block = (per_column, features // HALVES)
    vmem = pl.BlockSpec(memory_space=pltpu.VMEM)
    in_hbm = pl.BlockSpec(memory_space=pltpu.HBM)
    found = pl.pallas_call(
        layer_kernel,
        out_shape=jax.ShapeDtypeStruct((2, *tokens.shape), half),
        in_specs=[in_hbm] * 6,
        out_specs=vmem,
        scratch_shapes=[
            pltpu.VMEM(tokens.shape, half),
            pltpu.VMEM(tokens.shape, half),
            pltpu.VMEM(expert_ids.shape[::-1], jnp.int32),
            pltpu.VMEM(gate_score.shape[::-1], full),
            pltpu.VMEM(gate_rows.shape, half),
            pltpu.VMEM((features, 2 * hidden_size), half),
            pltpu.VMEM(down_weights.shape, half),
            pltpu.VMEM((2, *piece), half),
            pltpu.VMEM((2, members, *piece), half),
            pltpu.VMEM((HALVES, half_rows, 2 * hidden_size), full),
            pltpu.VMEM((HALVES, half_rows, hidden_size), full),
            pltpu.VMEM((HALVES, half_rows, 2 * hidden_size), half),
            pltpu.VMEM((HALVES, half_rows, hidden_size), half),
            pltpu.VMEM((HALVES, half_rows, 2 * hidden_size), half),
            pltpu.VMEM((HALVES, half_rows, hidden_size), half),
            pltpu.VMEM((half_rows, hidden_size), half),
            pltpu.VMEM((half_rows, 2 * hidden_size), half),
            pltpu.VMEM((2, HALVES, members, *block), half),
            pltpu.VMEM((2, HALVES, lines, *block), half),
            pltpu.VMEM((2, HALVES, HALVES, *block), half),
            pltpu.VMEM((2, HALVES, lines // HALVES, *block), half),
            pltpu.VMEM((2, HALVES, lines - 1, *block), half),
            pltpu.VMEM((2, HALVES, *block), half),
            pltpu.VMEM((2, *piece), half),
            pltpu.VMEM((members * per_column, 1), full),
            pltpu.VMEM((per_column, per_column), half),
            dma((4,)), dma((chunks,)), dma(()), dma((2,)), dma((2,)),
            dma((3, 2, members, groups)), dma((2, members, groups)),
            dma((lines // HALVES, 2)), dma((lines // HALVES, 2)),
            dma((2,)), dma((2,)), dma((HALVES,)), dma((HALVES,)),
            dma((2, HALVES, lines)), dma((2, HALVES, lines)),
            dma((2, HALVES, lines - 1)), dma((2, HALVES, HALVES)),
            dma((2, HALVES, lines // HALVES)),
            dma((2, HALVES)), dma((2, HALVES)),
        ],
        compiler_params=pltpu.CompilerParams(
            collective_id=0, has_side_effects=True, vmem_limit_bytes=48 << 20
        ),
        name="layer",
    )(*[
        pltpu.with_memory_space_constraint(value, pltpu.HBM)
        for value in (
            tokens, grad_out, jnp.transpose(expert_ids), jnp.transpose(gate_score),
            gate_rows, down_weights,
        )
    ])
    return found[0], found[1]


def on_device(tokens, grad_out, expert_ids, gate_score, w_gate_up, w_down):
    groups = lax.axis_size("group")
    members = lax.axis_size("expert")
    my_group = lax.axis_index("group")
    my_index = lax.axis_index("expert")
    per_column = tokens.shape[0]
    features = tokens.shape[1]
    visitors = per_column // 2
    top_count = expert_ids.shape[1]
    arrivals = groups * visitors
    capacity = min(arrivals, (3 * per_column * top_count + 2 * members - 1) // (2 * members))
    expert_rows = members * capacity
    weights = route_weights(gate_score).reshape(groups, members, per_column, top_count)
    pick_ids = expert_ids.reshape(groups, members, per_column, top_count)
    group_range = jnp.arange(groups, dtype=jnp.int32)
    my_picks = pick_ids[my_group, my_index]
    visits_mine = jnp.any(my_picks[:, :, None] // members == group_range, axis=1)
    leave_table = slot_matrix(visits_mine, visitors).astype(jnp.bfloat16)
    visits_here = jnp.any(pick_ids // members == my_group, axis=3)
    arrival_table = slot_matrix(visits_here[..., None], visitors)[:, :, 0]
    row_ids = jnp.einsum(
        "gest,getk->gesk", arrival_table, pick_ids.astype(jnp.float32), precision=HIGHEST
    )
    row_weights = jnp.einsum("gest,getk->gesk", arrival_table, weights, precision=HIGHEST)
    targets = (my_group * members + jnp.arange(members, dtype=jnp.int32)).astype(jnp.float32)
    matched = row_ids[..., None] == targets
    picked = jnp.any(matched, axis=3)
    picked_weight = jnp.sum(jnp.where(matched, row_weights[..., None], 0.0), axis=3)
    send_flags = picked[:, my_index].reshape(arrivals, members)
    send_table = slot_matrix(send_flags, capacity)
    send_share = jnp.transpose(picked_weight[:, my_index].reshape(arrivals, members))
    send_weight = send_table * send_share[:, None, :]
    came_flags = jnp.transpose(picked[:, :, :, my_index], (1, 0, 2)).reshape(members, arrivals)
    came_table = slot_matrix(came_flags[..., None], capacity)[:, 0]
    came_share = jnp.transpose(picked_weight[:, :, :, my_index], (1, 0, 2)).reshape(
        members, arrivals
    )
    slot_weight = jnp.einsum("ecr,er->ec", came_table, came_share, precision=HIGHEST).reshape(
        expert_rows
    )

    def dispatch(values):
        leaving = jnp.einsum(
            "gst,tf->gsf", leave_table, values, preferred_element_type=jnp.float32
        ).astype(jnp.bfloat16)
        arrived = across(leaving).reshape(arrivals, features)
        onward = jnp.einsum(
            "ecr,rf->ecf",
            send_table.astype(jnp.bfloat16),
            arrived,
            preferred_element_type=jnp.float32,
        ).astype(jnp.bfloat16)
        return within(onward).reshape(expert_rows, features)

    def combine(values, table):
        returned = within(values.reshape(members, capacity, features)).astype(jnp.float32)
        summed = jnp.einsum("ecr,ecf->rf", table, returned, precision=HIGHEST).astype(jnp.bfloat16)
        home = across(summed.reshape(groups, visitors, features))
        return jnp.einsum(
            "gst,gsf->tf", leave_table, home, preferred_element_type=jnp.float32
        ).astype(jnp.bfloat16)

    rows_in = dispatch(tokens)
    rows_grad = dispatch(grad_out)
    gate_weights = w_gate_up[0]
    down_weights = w_down[0]
    partial_value = jnp.einsum(
        "rf,fkh->rkh", rows_in, gate_weights, preferred_element_type=jnp.float32
    )
    grad_partial = jnp.einsum(
        "rf,hf->rh", rows_grad, down_weights, preferred_element_type=jnp.float32
    )
    empty_rows = jnp.zeros((expert_rows, features), jnp.float32)
    gate_both = share_sum(partial_value)
    gate_pre = gate_both[:, 0]
    up_pre = gate_both[:, 1]
    hidden = (jax.nn.silu(gate_pre) * up_pre).astype(jnp.bfloat16)[:, None, :]

    def down_step(running_sum, gathered, first_row):
        return jnp.dot(gathered[:, 0], down_weights, preferred_element_type=jnp.float32)

    expert_out = share_fold(hidden, down_step, empty_rows).astype(jnp.bfloat16)
    hidden_grad = share_sum(grad_partial[:, None, :])[:, 0] * slot_weight[:, None]
    pre_grad = local_grad(gate_pre, up_pre, hidden_grad)

    def input_step(running_sum, gathered, first_row):
        return jnp.einsum("rkh,fkh->rf", gathered, gate_weights, preferred_element_type=jnp.float32)

    expert_grad = share_fold(pre_grad, input_step, empty_rows).astype(jnp.bfloat16)
    layer_out = combine(expert_out, send_weight)
    grad_in = combine(expert_grad, send_table)
    return (layer_out, grad_in)


def per_device(tokens, grad_out, expert_ids, gate_score, w_gate_up, w_down):
    members = lax.axis_size("expert")
    dense = (
        expert_ids.shape[1] == members
        and members == LINES * LANES
        and lax.axis_size("group") == 2
        and lax.axis_size("dp") == 2
        and tokens.shape[0] == 2 * STRIP
        and expert_ids.shape[0] % SPAN == 0
        and tokens.shape[1] % (2 * TILE) == 0
        and w_gate_up.shape[3] % TILE == 0
    )
    plan = dense_device if dense else on_device
    return plan(tokens, grad_out, expert_ids, gate_score, w_gate_up, w_down)


def solution(mesh):
    return jax.shard_map(
        per_device,
        mesh=mesh,
        in_specs=(
            P(("group", "expert"), "dp"),
            P(("group", "expert"), "dp"),
            P(),
            P(),
            P(("group", "expert"), "dp", None, None),
            P(("group", "expert"), None, "dp"),
        ),
        out_specs=(P(("group", "expert"), "dp"), P(("group", "expert"), "dp")),
        check_vma=False,
    )
```
